256 devices in a mesh: grp: 8 (over y, x_lo), dev: 32 (over z, x_hi, core).
Axes of the slice: x: 4 (x_hi: 2, x_lo: 2; x = x_hi * 2 + x_lo), y: 4, z: 8, core: 2. Of those that a mesh axis runs over, the one named last changes fastest.
Arguments:
- border: bfloat16 [8, 131072, 1024], P('grp', 'dev'), may hold values from -1.5 to 1.5
- inverse_blocks: bfloat16 [8, 1024, 1024], P('grp')
- selected: int32 [256], replicated, may hold values from 0 to 131071, as said below
- assignment: int32 [8], replicated, may hold values from 0 to 7, each once
- probability: float32 [8], replicated, may hold values from 2 to 8
- prior_panel: bfloat16 [131072, 256], P(('dev', 'grp'))
Outputs:
- panel_out: float32 [131072, 256], P(('dev', 'grp'))
- residual: float32 [8, 1024, 256], P('grp', 'dev')
The draws below stay inside these ranges and needn't reach their ends.
Inputs may be any that keep to these rules, and one draw needn't show every extreme that they name: `selected`: 256 distinct rows.
All inputs are finite; a program needn't handle non-finite values.
Results may differ from the reference program's by a relative error of at most 0.0005.
The reference program's roundings to bfloat16 on the way (of `picked`, `project` and `rounded`) count: a program that leaves them out, or rounds other values in their place, can miss the bound.
Values may be sent and summed in bfloat16 or wider, within the bound.
A program may use at most 64 MiB of HBM per device.

```python
import math
import jax
import jax.numpy as jnp
from jax import lax

N1 = 131072
E = 1024
W = 256
GROUPS = 8


def choose_rows(key):
    order = jax.random.permutation(jax.random.fold_in(key, 11), N1)
    return order[:W].astype(jnp.int32)


def draw_selected(key, part):
    return choose_rows(key)


def draw_prior_panel(key, part):
    rows_taken = choose_rows(key)
    values = jax.random.normal(jax.random.fold_in(key, 12), (N1, W), jnp.float32)
    marked = jnp.any(jnp.arange(N1, dtype=jnp.int32)[:, None] == rows_taken[None, :], axis=1)
    scales = jnp.where(marked, 0.1875, 20.0)
    return (values * scales[:, None]).astype(jnp.bfloat16)


def draw_inverse_blocks(key, part):
    factors = jax.random.normal(jax.random.fold_in(key, 21), (GROUPS, E, E), jnp.float32) / jnp.sqrt(E * 1.0)
    spread = jnp.einsum('gij,gkj->gik', factors, factors) + 0.5 * jnp.eye(E, dtype=jnp.float32)[None, :, :]
    return spread.astype(jnp.bfloat16)


def shard_levels(rng, dims, shards, smallest, largest):
    gain, own = 1.0, jax.random.fold_in(rng, 6)
    for dim, shards_of in shards:
        draws = jnp.exp(jax.random.uniform(jax.random.fold_in(own, dim), (shards_of,), jnp.float32, smallest / len(shards), largest / len(shards)))
        gain = gain * jnp.repeat(draws, dims[dim] // shards_of).reshape([-1 if axis == dim else 1 for axis in range(len(dims))])
    return gain


def noise(key, shape, deviation, limit, cuts=(), kind=jnp.bfloat16):
    entries = deviation * jax.random.normal(key, shape, jnp.float32)
    if cuts:
        entries = entries * shard_levels(key, shape, cuts, -0.22, 0.18)
    return jnp.clip(entries, -limit, limit).astype(kind)


def setup_inputs(seed: int = 0) -> dict:
    splits = jax.random.split(jax.random.key(seed), 7)
    return {
        "border": noise(splits[0], (GROUPS, N1, E), 0.25, 1.5, ((0, 8), (1, 32))),
        "inverse_blocks": draw_inverse_blocks(jax.random.fold_in(splits[6], 71), 0),
        "selected": draw_selected(jax.random.fold_in(splits[6], 71), 0),
        "assignment": jax.random.permutation(splits[3], GROUPS).astype(jnp.int32),
        "probability": jnp.clip(jnp.exp(jax.random.uniform(splits[4], (GROUPS,), jnp.float32, math.log(2.0), math.log(8.0))), 2.0, 8.0),
        "prior_panel": draw_prior_panel(jax.random.fold_in(splits[6], 71), 0),
    }


def reference(border, inverse_blocks, selected, assignment, probability, prior_panel):
    groups = border.shape[0]
    rank_list = jnp.arange(groups, dtype=jnp.int32)
    weights = lax.optimization_barrier(jnp.sum(jnp.where(assignment[:, None] == rank_list[None, :], probability[None, :], 0.0), axis=1))

    def add_group(schur_sum, members):
        scenario_rows, inverse, weight = members
        picked = jnp.take(scenario_rows, selected, axis=0)
        project = lax.dot_general(inverse.astype(jnp.float32), picked.astype(jnp.float32), (((1,), (1,)), ((), ())), preferred_element_type=jnp.float32).astype(jnp.bfloat16)
        return (schur_sum + weight * jnp.dot(scenario_rows.astype(jnp.float32), project.astype(jnp.float32), preferred_element_type=jnp.float32), None)
    schur_sum, unused = lax.scan(add_group, jnp.zeros((N1, W), jnp.float32), (border, inverse_blocks, weights))
    prior_sel = jnp.take(prior_panel, selected, axis=0)
    schur_panel = schur_sum - lax.dot_general(prior_panel.astype(jnp.float32), prior_sel.astype(jnp.float32), (((1,), (1,)), ((), ())), preferred_element_type=jnp.float32)
    corner = jnp.take(schur_panel, selected, axis=0)
    factor = jnp.linalg.cholesky(corner)
    solved = jax.scipy.linalg.solve_triangular(factor, schur_panel.T, lower=True).T
    marked = jnp.any(jnp.arange(N1, dtype=jnp.int32)[:, None] == selected[None, :], axis=1)
    panel_out = jnp.where(marked[:, None], 0.0, solved)
    rounded = panel_out.astype(jnp.bfloat16)

    def group_product(scenario_rows):
        return lax.dot_general(scenario_rows.astype(jnp.float32), rounded.astype(jnp.float32), (((0,), (0,)), ((), ())), preferred_element_type=jnp.float32) / math.sqrt(N1)
    residual = lax.map(group_product, border)
    return (panel_out, residual)
```

```python
import functools
import math

import jax
import jax.numpy as jnp
from jax import lax
from jax.experimental import pallas as pl
from jax.experimental.pallas import tpu as pltpu
from jax.sharding import PartitionSpec as P

N1 = 131072
MESH = pl.DeviceIdType.MESH
HIGHEST = lax.Precision.HIGHEST
F32 = jnp.float32
BF16 = jnp.bfloat16
LANES = 128
CORES, XHI = 2, 2
TOP = 32767.0


def params(collective_id, limit=60):
    return pltpu.CompilerParams(
        collective_id=collective_id, has_side_effects=True, vmem_limit_bytes=limit << 20
    )


def dot(a, b, ca, cb, precision=None):
    return lax.dot_general(
        a, b, (((ca,), (cb,)), ((), ())), precision=precision, preferred_element_type=F32
    )


def meet(partners):
    barrier = pltpu.get_barrier_semaphore()
    for where in partners:
        pl.semaphore_signal(barrier, inc=1, device_id=where, device_id_type=MESH)
    pl.semaphore_wait(barrier, len(partners))


def remote(src, dst, send, recv, where):
    return pltpu.make_async_remote_copy(
        src_ref=src, dst_ref=dst, send_sem=send, recv_sem=recv, device_id=where, device_id_type=MESH
    )


def dev_partners(grp, dev, count):
    depth = count // (CORES * XHI)
    per = CORES * XHI
    z, rest = dev // per, dev % per
    xhi, core = rest // CORES, rest % CORES
    at = lambda zz, xx, cc: (grp, (zz * XHI + xx) * CORES + cc)
    others = [at((z + o) % depth, xhi, core) for o in range(1, depth)]
    return z, xhi, core, at(z, xhi, 1 - core), at(z, 1 - xhi, core), others


def rows_kernel(
    groups, count, border, prior, sel, out,
    big, flat, got1, got2, got3, load, send1, recv1, send2, recv2, send3, recv3, send4, recv4, send5, recv5, send6, recv6,
):
    grp, dev = lax.axis_index("grp"), lax.axis_index("dev")
    z, xhi, core, cpart, xpart, zparts = dev_partners(grp, dev, count)
    depth = count // (CORES * XHI)
    pieces, height = big.shape[0], big.shape[1]
    width, own = sel.shape[0], prior.shape[0]
    for i in range(pieces):
        pltpu.make_async_copy(border.at[pl.ds(i * height, height)], big.at[i], load.at[i]).start()
    meet([cpart, xpart] + zparts)
    want = sel[...][:, :1]
    first = (dev * groups + grp) * own
    hot = (want - first == lax.broadcasted_iota(jnp.int32, (width, own), 1)).astype(F32).astype(BF16)
    total = flat.shape[0]
    cols = (total - 2 * width) // width
    mine = dot(hot, prior[...], 1, 0).astype(BF16)
    for c in range(2):
        flat[pl.ds((cols + c) * width, width), :] = mine[:, c * LANES : (c + 1) * LANES]
    acc = None
    for i in range(pieces):
        pltpu.make_async_copy(border.at[pl.ds(i * height, height)], big.at[i], load.at[i]).wait()
        base = dev * (pieces * height) + i * height
        hot = (want - base == lax.broadcasted_iota(jnp.int32, (width, height), 1)).astype(F32).astype(BF16)
        part = dot(hot, big[i], 1, 0)
        acc = part if acc is None else acc + part
    acc = acc.astype(BF16)
    for c in range(cols):
        flat[pl.ds(c * width, width), :] = acc[:, c * LANES : (c + 1) * LANES]
    half, quarter, part = total // CORES, total // (CORES * XHI), total // count
    go = remote(flat.at[pl.ds((1 - core) * half, half)], got1, send1, recv1, cpart)
    go.start()
    go.wait()
    at1 = core * half
    flat[pl.ds(at1, half), :] = flat[pl.ds(at1, half), :] + got1[...]
    go = remote(flat.at[pl.ds(at1 + (1 - xhi) * quarter, quarter)], got2, send2, recv2, xpart)
    go.start()
    go.wait()
    at2 = at1 + xhi * quarter
    flat[pl.ds(at2, quarter), :] = flat[pl.ds(at2, quarter), :] + got2[...]
    gos = []
    for o in range(1, depth):
        there = (z + o) % depth
        go = remote(flat.at[pl.ds(at2 + there * part, part)], got3.at[o - 1], send3.at[o - 1], recv3.at[o - 1], zparts[o - 1])
        go.start()
        gos.append(go)
    at3 = at2 + z * part
    value = flat[pl.ds(at3, part), :]
    for o in range(1, depth):
        gos[o - 1].wait_recv()
        value = value + got3[o - 1]
    out[pl.ds(at3, part), :] = value
    outs = []
    for o in range(1, depth):
        go = remote(out.at[pl.ds(at3, part)], out.at[pl.ds(at3, part)], send4.at[o - 1], recv4.at[o - 1], zparts[o - 1])
        go.start()
        outs.append(go)
    for o in range(1, depth):
        there = at2 + ((z + depth - o) % depth) * part
        remote(out.at[pl.ds(there, part)], out.at[pl.ds(there, part)], send4.at[o - 1], recv4.at[o - 1], zparts[o - 1]).wait_recv()
    go = remote(out.at[pl.ds(at2, quarter)], out.at[pl.ds(at2, quarter)], send5, recv5, xpart)
    go.start()
    outs.append(go)
    other = at1 + (1 - xhi) * quarter
    remote(out.at[pl.ds(other, quarter)], out.at[pl.ds(other, quarter)], send5, recv5, xpart).wait_recv()
    go = remote(out.at[pl.ds(at1, half)], out.at[pl.ds(at1, half)], send6, recv6, cpart)
    go.start()
    outs.append(go)
    other = (1 - core) * half
    remote(out.at[pl.ds(other, half)], out.at[pl.ds(other, half)], send6, recv6, cpart).wait_recv()
    for go in gos + outs:
        go.wait_send()


def rows_call(groups, count, border, prior, sel):
    rows, size = border.shape
    width = sel.shape[0]
    total = (size // LANES + 2) * width
    depth = count // (CORES * XHI)
    height = min(512, rows)
    dma = pltpu.SemaphoreType.DMA
    vm = pl.BlockSpec(memory_space=pltpu.VMEM)
    n = max(depth - 1, 1)
    return pl.pallas_call(
        functools.partial(rows_kernel, groups, count),
        out_shape=jax.ShapeDtypeStruct((total, LANES), BF16),
        in_specs=[pl.BlockSpec(memory_space=pl.ANY), vm, vm],
        out_specs=vm,
        scratch_shapes=[
            pltpu.VMEM((rows // height, height, size), BF16),
            pltpu.VMEM((total, LANES), BF16),
            pltpu.VMEM((total // CORES, LANES), BF16),
            pltpu.VMEM((total // (CORES * XHI), LANES), BF16),
            pltpu.VMEM((n, total // count, LANES), BF16),
            dma((rows // height,)),
            dma, dma, dma, dma, dma((n,)), dma((n,)), dma((n,)), dma((n,)), dma, dma, dma, dma,
        ],
        compiler_params=params(0),
        name="rows",
    )(border, prior, sel)


def refine(d):
    r = 1.0 / d
    return r * (2.0 - d * r)


def eliminate(work, inv):
    size = work.shape[0]
    lane = lax.broadcasted_iota(jnp.int32, (8, 2 * size), 1)
    row = lax.broadcasted_iota(jnp.int32, (8, 2 * size), 0)

    def panel(p, carry):
        at = pl.multiple_of(p * 8, 8)
        block = work[pl.ds(at, 8), :]
        near = pltpu.roll(block, (2 * size - at) % (2 * size), axis=1)
        cs = [jnp.broadcast_to(near[:, j : j + 1], (8, 2 * size)) for j in range(8)]
        pivots = jnp.zeros((8, 2 * size), F32)
        for j in range(8):
            pivots = jnp.where(row == j, cs[j], pivots)
            d = jnp.broadcast_to(cs[j][j : j + 1, :], (8, 2 * size))
            m = jnp.where(row > j, cs[j] * refine(d), 0.0)
            block = block - m * jnp.broadcast_to(block[j : j + 1, :], (8, 2 * size))
            for k in range(j + 1, 8):
                cs[k] = cs[k] - m * jnp.broadcast_to(cs[k][j : j + 1, :], (8, 2 * size))
        r = lax.rsqrt(pivots)
        r = r * (1.5 - 0.5 * pivots * r * r)
        inv[pl.ds(at, 8), :] = (block * r)[:, size:]
        scaled = jnp.where((lane >= at + 8) & (lane < size), block * refine(pivots), 0.0)
        turned = jnp.transpose(scaled)[:size, :]
        rest = work[...]
        for j in range(8):
            rest = rest - jnp.broadcast_to(turned[:, j : j + 1], rest.shape) * jnp.broadcast_to(block[j : j + 1, :], rest.shape)
        work[...] = rest
        return carry

    lax.fori_loop(0, size // 8, panel, 0)


def inverse_factor(a, work, inv):
    n = a.shape[0]
    base = work.shape[0]
    if n == base:
        i = lax.broadcasted_iota(jnp.int32, (n, n), 0)
        j = lax.broadcasted_iota(jnp.int32, (n, n), 1)
        work[...] = jnp.concatenate([a, (i == j).astype(F32)], axis=1)
        eliminate(work, inv)
        return inv[...]
    h = n // 2
    w11 = inverse_factor(a[:h, :h], work, inv)
    l21 = dot(a[h:, :h], w11, 1, 1, HIGHEST)
    w22 = inverse_factor(a[h:, h:] - dot(l21, l21, 1, 1, HIGHEST), work, inv)
    w21 = -dot(dot(w22, l21, 1, 0, HIGHEST), w11, 1, 0, HIGHEST)
    top = jnp.concatenate([w11, jnp.zeros((h, h), F32)], axis=1)
    return jnp.concatenate([top, jnp.concatenate([w21, w22], axis=1)], axis=0)


def schur_kernel(
    groups, border, inverse, flat, prior, sel, asg, prob, panel, rounded,
    big, minv, fl, picked, project, corner, corner_got, corner_sum, q_got, q, code, code_got, scale, scale_got, work, invb,
    load, send, recv,
):
    grp, dev = lax.axis_index("grp"), lax.axis_index("dev")
    order = [o for o in (5, 7, 3, 4, 1, 6, 2) if o < groups]
    parts = {o: (grp ^ o, dev) for o in order}
    width = picked.shape[0]
    size = picked.shape[1]
    own = prior.shape[0]
    loads = [
        pltpu.make_async_copy(flat, fl, load.at[groups]),
        pltpu.make_async_copy(inverse, minv, load.at[groups + 1]),
    ] + [
        pltpu.make_async_copy(border.at[pl.ds((grp ^ o) * own, own)], big.at[o], load.at[o])
        for o in order + [0]
    ]
    for go in loads:
        go.start()
    meet([parts[o] for o in order])
    scenario = asg[grp]
    weight = 0.0
    for i in range(groups):
        weight = weight + jnp.where(scenario == i, prob[i], 0.0)
    loads[0].wait()
    for c in range(size // LANES):
        picked[:, c * LANES : (c + 1) * LANES] = fl[pl.ds(c * width, width), :]
    qbase = (size // LANES) * width
    gos = []

    def go_to(kind, o, src, dst):
        go = remote(src, dst, send.at[kind, o - 1], recv.at[kind, o - 1], parts[o])
        go.start()
        gos.append(go)

    def landed(kind, o, dst):
        remote(dst, dst, send.at[kind, o - 1], recv.at[kind, o - 1], parts[o]).wait_recv()

    qpart = (2 * width) // groups
    for o in order:
        go_to(0, o, fl.at[pl.ds(qbase + (grp ^ o) * qpart, qpart)], q_got.at[o])
    loads[1].wait()
    project[...] = dot(minv[...], picked[...], 1, 1).astype(BF16)
    corner[...] = weight * dot(picked[...], project[...], 1, 0)
    cpart = width // groups
    for o in order:
        go_to(1, o, corner.at[pl.ds((grp ^ o) * cpart, cpart)], corner_got.at[o])
    for o in order:
        landed(0, o, q_got.at[o])
    mine = fl[pl.ds(qbase + grp * qpart, qpart), :]
    for o in order:
        mine = mine + q_got[o]
    q[pl.ds(grp * qpart, qpart), :] = mine
    for o in order:
        here = q.at[pl.ds(grp * qpart, qpart)]
        go_to(2, o, here, here)
    first = True
    for n, o in enumerate(order):
        loads[2 + n].wait()
        block = weight * jnp.dot(big[o], project[...], preferred_element_type=F32)
        peak = jnp.maximum(jnp.max(jnp.abs(block), axis=0, keepdims=True), 1e-30)
        x = block * (TOP / peak)
        code[o] = jnp.round(x).astype(jnp.int32).astype(jnp.int16)
        scale[o] = jnp.broadcast_to(peak * (1.0 / TOP), scale.shape[1:])
        go_to(4, o, scale.at[o], scale_got.at[o])
        go_to(5, o, code.at[o], code_got.at[o])
        if first:
            first = False
            for k in order:
                landed(1, k, corner_got.at[k])
            mine = corner[pl.ds(grp * cpart, cpart), :]
            for k in order:
                mine = mine + corner_got[k]
            corner_sum[pl.ds(grp * cpart, cpart), :] = mine
            for k in order:
                here = corner_sum.at[pl.ds(grp * cpart, cpart)]
                go_to(3, k, here, here)
    loads[-1].wait()
    panel[...] = weight * jnp.dot(big[0], project[...], preferred_element_type=F32)
    for o in order:
        there = pl.ds((grp ^ o) * qpart, qpart)
        landed(2, o, q.at[there])
        there = pl.ds((grp ^ o) * cpart, cpart)
        landed(3, o, corner_sum.at[there])
    qs = jnp.concatenate([q[pl.ds(c * width, width), :] for c in range(2)], axis=1)
    a = corner_sum[...] - dot(qs, qs, 1, 1)
    a = 0.5 * (a + jnp.transpose(a))
    w = inverse_factor(a, work, invb)
    total = panel[...] - dot(prior[...], qs, 1, 1)
    for o in order:
        landed(4, o, scale_got.at[o])
        landed(5, o, code_got.at[o])
        total = total + code_got[o].astype(jnp.int32).astype(F32) * scale_got[o][:1, :]
    solved = dot(total, w, 1, 1, HIGHEST)
    ids = (dev * groups + grp) * own + lax.broadcasted_iota(jnp.int32, (own, width), 0)
    hit = jnp.max((ids == sel[...]).astype(F32), axis=1, keepdims=True)
    solved = jnp.where(hit > 0.5, 0.0, solved)
    panel[...] = solved
    rounded[...] = solved.astype(BF16)
    for go in gos:
        go.wait_send()


def schur_call(groups, border, inverse, flat, prior, sel, asg, prob):
    rows, size = border.shape
    own, width = prior.shape
    dma = pltpu.SemaphoreType.DMA
    vm = pl.BlockSpec(memory_space=pltpu.VMEM)
    anyspace = pl.BlockSpec(memory_space=pl.ANY)
    sm = pl.BlockSpec(memory_space=pltpu.SMEM)
    base = 64
    return pl.pallas_call(
        functools.partial(schur_kernel, groups),
        out_shape=(jax.ShapeDtypeStruct((own, width), F32), jax.ShapeDtypeStruct((own, width), BF16)),
        in_specs=[anyspace, anyspace, anyspace, vm, vm, sm, sm],
        out_specs=(vm, vm),
        scratch_shapes=[
            pltpu.VMEM((groups, own, size), BF16),
            pltpu.VMEM((size, size), BF16),
            pltpu.VMEM(flat.shape, BF16),
            pltpu.VMEM((width, size), BF16),
            pltpu.VMEM((size, width), BF16),
            pltpu.VMEM((width, width), F32),
            pltpu.VMEM((groups, width // groups, width), F32),
            pltpu.VMEM((width, width), F32),
            pltpu.VMEM((groups, 2 * width // groups, LANES), BF16),
            pltpu.VMEM((2 * width, LANES), BF16),
            pltpu.VMEM((groups, own, width), jnp.int16),
            pltpu.VMEM((groups, own, width), jnp.int16),
            pltpu.VMEM((groups, 8, width), F32),
            pltpu.VMEM((groups, 8, width), F32),
            pltpu.VMEM((base, 2 * base), F32),
            pltpu.VMEM((base, base), F32),
            dma((groups + 2,)),
            dma((6, groups - 1)),
            dma((6, groups - 1)),
        ],
        compiler_params=params(1),
        name="schur",
    )(border, inverse, flat, prior, sel, asg, prob)


def products_kernel(
    groups, count, border, rounded, out,
    big, panel, acc, sums, got1, keep1, got2, keep2, got3, load, send, recv, send1, recv1, send2, recv2, send3, recv3,
):
    grp, dev = lax.axis_index("grp"), lax.axis_index("dev")
    z, xhi, core, cpart, xpart, zparts = dev_partners(grp, dev, count)
    depth = count // (CORES * XHI)
    order = [o for o in (5, 7, 3, 4, 1, 6, 2) if o < groups]
    own = rounded.shape[0]
    loads = [
        pltpu.make_async_copy(border.at[pl.ds((grp ^ o) * own, own)], big.at[o], load.at[o])
        for o in [0] + order[::-1]
    ]
    for go in loads:
        go.start()
    meet([(grp ^ o, dev) for o in order] + [cpart, xpart] + zparts)
    gos = []
    for o in order:
        go = remote(rounded, panel.at[o], send.at[o - 1], recv.at[o - 1], (grp ^ o, dev))
        go.start()
        gos.append(go)
    loads[0].wait()
    acc[...] = dot(rounded[...], big[0], 0, 0)
    for n, o in enumerate(order[::-1]):
        loads[1 + n].wait()
        gos[len(order) - 1 - n].wait_recv()
        acc[...] += dot(panel[o], big[o], 0, 0)
    width = acc.shape[0]
    piece = sums.shape[3]
    scale = 1.0 / math.sqrt(N1)
    for e in range(acc.shape[1] // LANES):
        turned = jnp.transpose(acc[:, e * LANES : (e + 1) * LANES]) * scale
        for k in range(LANES // piece):
            at = e * (LANES // piece) + k
            zz, xx, cc = at // (XHI * CORES), (at // CORES) % XHI, at % CORES
            sums[cc, zz, xx] = turned[k * piece : (k + 1) * piece, :]
    go = remote(sums.at[1 - core], got1, send1, recv1, cpart)
    go.start()
    gos.append(go)
    go.wait_recv()
    for x in range(XHI):
        for zz in range(depth):
            keep1[x, zz] = sums[core, zz, x] + got1[zz, x]
    go = remote(keep1.at[1 - xhi], got2, send2, recv2, xpart)
    go.start()
    gos.append(go)
    go.wait_recv()
    keep2[...] = keep1[xhi] + got2[...]
    last = []
    for o in range(1, depth):
        go = remote(keep2.at[(z + o) % depth], got3.at[o - 1], send3.at[o - 1], recv3.at[o - 1], zparts[o - 1])
        go.start()
        last.append(go)
    value = keep2[z]
    for o in range(1, depth):
        last[o - 1].wait_recv()
        value = value + got3[o - 1]
    out[...] = value
    for go in gos + last:
        go.wait_send()


def products_call(groups, count, border, rounded):
    rows, size = border.shape
    own, width = rounded.shape
    piece = size // count
    depth = count // (CORES * XHI)
    n = max(depth - 1, 1)
    dma = pltpu.SemaphoreType.DMA
    vm = pl.BlockSpec(memory_space=pltpu.VMEM)
    return pl.pallas_call(
        functools.partial(products_kernel, groups, count),
        out_shape=jax.ShapeDtypeStruct((piece, width), F32),
        in_specs=[pl.BlockSpec(memory_space=pl.ANY), vm],
        out_specs=vm,
        scratch_shapes=[
            pltpu.VMEM((groups, own, size), BF16),
            pltpu.VMEM((groups, own, width), BF16),
            pltpu.VMEM((width, size), F32),
            pltpu.VMEM((CORES, depth, XHI, piece, width), F32),
            pltpu.VMEM((depth, XHI, piece, width), F32),
            pltpu.VMEM((XHI, depth, piece, width), F32),
            pltpu.VMEM((depth, piece, width), F32),
            pltpu.VMEM((depth, piece, width), F32),
            pltpu.VMEM((n, piece, width), F32),
            dma((groups,)), dma((groups - 1,)), dma((groups - 1,)), dma, dma, dma, dma, dma((n,)), dma((n,)),
        ],
        compiler_params=params(2),
        name="products",
    )(border, rounded)


def body(border, inverse_blocks, selected, assignment, probability, prior_panel):
    groups, count = lax.axis_size("grp"), lax.axis_size("dev")
    mine = border[0]
    column = jnp.broadcast_to(selected[:, None], (selected.shape[0], LANES))
    flat = rows_call(groups, count, mine, prior_panel, column)
    panel, rounded = schur_call(
        groups, mine, inverse_blocks[0], flat, prior_panel, selected[None, :], assignment, probability
    )
    residual = products_call(groups, count, mine, rounded)
    return (panel, residual[None])


def solution(mesh):
    return jax.shard_map(
        body,
        mesh=mesh,
        in_specs=(
            P("grp", "dev", None),
            P("grp", None, None),
            P(),
            P(),
            P(),
            P(("dev", "grp"), None),
        ),
        out_specs=(P(("dev", "grp"), None), P("grp", "dev", None)),
        check_vma=False,
    )
```

```python
import functools
import math

import jax
import jax.numpy as jnp
from jax import lax
from jax.experimental import pallas as pl
from jax.experimental.pallas import tpu as pltpu
from jax.sharding import PartitionSpec as P

N1 = 131072
MESH = pl.DeviceIdType.MESH
HIGHEST = lax.Precision.HIGHEST
F32 = jnp.float32
BF16 = jnp.bfloat16
I16 = jnp.int16
LANES = 128
CORES, XHI, XLO = 2, 2, 2
TOP = 32767.0
BASE = 64


def dot(a, b, ca, cb, precision=None):
    return lax.dot_general(
        a, b, (((ca,), (cb,)), ((), ())), precision=precision, preferred_element_type=F32
    )


def split(own, share):
    part = max(16, int(own * share / 16 + 0.5) * 16)
    return own - part, part


def encode(x, code, scale):
    peak = jnp.maximum(jnp.max(jnp.abs(x), axis=0, keepdims=True), 1e-30)
    code[...] = jnp.round(x * (TOP / peak)).astype(jnp.int32).astype(I16)
    scale[...] = peak * (1.0 / TOP)


def decode(code, scale):
    return code.astype(jnp.int32).astype(F32) * scale


def refine(d):
    r = 1.0 / d
    return r * (2.0 - d * r)


def eliminate(work, inv):
    size = work.shape[0]
    lane = lax.broadcasted_iota(jnp.int32, (8, 2 * size), 1)
    row = lax.broadcasted_iota(jnp.int32, (8, 2 * size), 0)

    def panel(p, carry):
        at = pl.multiple_of(p * 8, 8)
        block = work[pl.ds(at, 8), :]
        near = pltpu.roll(block, (2 * size - at) % (2 * size), axis=1)
        cs = [jnp.broadcast_to(near[:, j : j + 1], (8, 2 * size)) for j in range(8)]
        pivots = jnp.zeros((8, 2 * size), F32)
        for j in range(8):
            pivots = jnp.where(row == j, cs[j], pivots)
            d = jnp.broadcast_to(cs[j][j : j + 1, :], (8, 2 * size))
            m = jnp.where(row > j, cs[j] * refine(d), 0.0)
            block = block - m * jnp.broadcast_to(block[j : j + 1, :], (8, 2 * size))
            for k in range(j + 1, 8):
                cs[k] = cs[k] - m * jnp.broadcast_to(cs[k][j : j + 1, :], (8, 2 * size))
        r = lax.rsqrt(pivots)
        r = r * (1.5 - 0.5 * pivots * r * r)
        inv[pl.ds(at, 8), :] = (block * r)[:, size:]
        scaled = jnp.where((lane >= at + 8) & (lane < size), block * refine(pivots), 0.0)
        turned = jnp.transpose(scaled)[:size, :]
        rest = work[...]
        for j in range(8):
            rest = rest - jnp.broadcast_to(turned[:, j : j + 1], rest.shape) * jnp.broadcast_to(block[j : j + 1, :], rest.shape)
        work[...] = rest
        return carry

    lax.fori_loop(0, size // 8, panel, 0)


def inverse_factor(a, work, inv, hooks):
    n = a.shape[0]
    if n == BASE:
        i = lax.broadcasted_iota(jnp.int32, (n, n), 0)
        j = lax.broadcasted_iota(jnp.int32, (n, n), 1)
        work[...] = jnp.concatenate([a, (i == j).astype(F32)], axis=1)
        eliminate(work, inv)
        if hooks:
            hooks.pop(0)()
        return inv[...]
    h = n // 2
    w11 = inverse_factor(a[:h, :h], work, inv, hooks)
    l21 = dot(a[h:, :h], w11, 1, 1, HIGHEST)
    w22 = inverse_factor(a[h:, h:] - dot(l21, l21, 1, 1, HIGHEST), work, inv, hooks)
    w21 = -dot(dot(w22, l21, 1, 0, HIGHEST), w11, 1, 0, HIGHEST)
    top = jnp.concatenate([w11, jnp.zeros((h, h), F32)], axis=1)
    return jnp.concatenate([top, jnp.concatenate([w21, w22], axis=1)], axis=0)


class Mail:
    def __init__(self, send, recv):
        self.send, self.recv, self.ids, self.started = send, recv, {}, []

    def copy(self, key, src, dst, where):
        k = self.ids.setdefault(key, len(self.ids))
        return pltpu.make_async_remote_copy(
            src_ref=src, dst_ref=dst, send_sem=self.send.at[k], recv_sem=self.recv.at[k],
            device_id=where, device_id_type=MESH,
        )

    def start(self, key, src, dst, where):
        go = self.copy(key, src, dst, where)
        go.start()
        self.started.append(go)

    def take(self, key, dst, where):
        self.copy(key, dst, dst, where).wait_recv()

    def close(self):
        for go in self.started:
            go.wait_send()


def kernel(
    groups, count, border, inverse, prior_hbm, sel, asg, prob, panel, out,
    big, minv, prior, flat, rows, got1, got2, got3, q0, qg, qs, qh, qx, qz, q, picked, project,
    corner, corner_got, corner_sum, ya, ya_s, ya_g, ya_sg, xb, xb_s, xb_g, xb_sg,
    xa, xa_s, xa_g, xa_sg, yb, yb_s, yb_g, yb_sg, keep0, keep_a, keep_b, hit, work, invb,
    pan, acc, sums, core_got, keep1, x_code, x_scale, x_got, x_sgot, keep2, z_code, z_scale, z_got, z_sgot,
    load, send, recv,
):
    grp, dev = lax.axis_index("grp"), lax.axis_index("dev")
    depth = count // (CORES * XHI)
    z, xhi, core = dev // (CORES * XHI), (dev // CORES) % XHI, dev % CORES
    at = lambda zz, xx, cc: (grp, (zz * XHI + xx) * CORES + cc)
    cpart, xpart = at(z, xhi, 1 - core), at(z, 1 - xhi, core)
    zparts = {o: at((z + o) % depth, xhi, core) for o in range(1, depth)}
    ys = [y for y in (2, 1, 3) if y < groups // XLO]
    near = [o for o in (5, 4, 7, 6, 3, 2, 1) if o < groups]
    peer = {o: (grp ^ o, dev) for o in near}
    width, size = picked.shape
    own = prior.shape[0]
    mail = Mail(send, recv)

    loads = {o: pltpu.make_async_copy(border.at[pl.ds((grp ^ o) * own, own)], big.at[o], load.at[o]) for o in range(groups)}
    loads["prior"] = pltpu.make_async_copy(prior_hbm, prior, load.at[groups])
    loads["inverse"] = pltpu.make_async_copy(inverse, minv, load.at[groups + 1])
    for name in ["prior"] + list(range(groups)) + ["inverse"]:
        loads[name].start()
    barrier = pltpu.get_barrier_semaphore()
    partners = [cpart, xpart] + list(zparts.values()) + list(peer.values())
    for where in partners:
        pl.semaphore_signal(barrier, inc=1, device_id=where, device_id_type=MESH)

    want = jnp.transpose(jnp.broadcast_to(sel[...], (LANES, width)))[:, :1]
    want = jnp.broadcast_to(want, (width, own))
    lanes = lax.broadcasted_iota(jnp.int32, (width, own), 1)
    first = (dev * groups + grp) * own
    loads["prior"].wait()
    mine = dot((want - first == lanes).astype(F32).astype(BF16), prior[...], 1, 0).astype(BF16)
    for c in range(2):
        q0[pl.ds(c * width, width), :] = mine[:, c * LANES : (c + 1) * LANES]
    total = None
    for o in range(groups):
        loads[o].wait()
        base = (dev * groups + (grp ^ o)) * own
        part = dot((want - base == lanes).astype(F32).astype(BF16), big[o], 1, 0)
        total = part if total is None else total + part
    total = total.astype(BF16)
    for c in range(size // LANES):
        flat[pl.ds(c * width, width), :] = total[:, c * LANES : (c + 1) * LANES]
    pl.semaphore_wait(barrier, len(partners))

    high = flat.shape[0]
    half, quarter, bit = high // CORES, high // (CORES * XHI), high // count
    qpart = (2 * width) // groups
    qhalf, qquart = qpart // CORES, qpart // (CORES * XHI)
    at1 = core * half
    at2 = at1 + xhi * quarter
    at3 = at2 + z * bit
    mail.start("r1", flat.at[pl.ds((1 - core) * half, half)], got1, cpart)
    for o in near:
        mail.start(("q0", o), q0.at[pl.ds((grp ^ o) * qpart, qpart)], qg.at[o], peer[o])
    mail.take("r1", got1, cpart)
    flat[pl.ds(at1, half), :] = flat[pl.ds(at1, half), :] + got1[...]
    mail.start("r2", flat.at[pl.ds(at1 + (1 - xhi) * quarter, quarter)], got2, xpart)
    ids = first + lax.broadcasted_iota(jnp.int32, (own, width), 0)
    marked = jnp.max((ids == sel[...]).astype(F32), axis=1, keepdims=True)
    hit[...] = jnp.broadcast_to(marked, hit.shape)
    value = q0[pl.ds(grp * qpart, qpart), :]
    for o in near:
        mail.take(("q0", o), qg.at[o], peer[o])
        value = value + qg[o]
    qs[...] = value
    mail.start("q1", qs.at[pl.ds((1 - core) * qhalf, qhalf)], qh, cpart)
    mail.take("r2", got2, xpart)
    flat[pl.ds(at2, quarter), :] = flat[pl.ds(at2, quarter), :] + got2[...]
    for o in range(1, depth):
        mail.start(("r3", o), flat.at[pl.ds(at2 + ((z + o) % depth) * bit, bit)], got3.at[o - 1], zparts[o])
    mail.take("q1", qh, cpart)
    qs[pl.ds(core * qhalf, qhalf), :] = qs[pl.ds(core * qhalf, qhalf), :] + qh[...]
    qat = core * qhalf + xhi * qquart
    mail.start("q2", qs.at[pl.ds(core * qhalf + (1 - xhi) * qquart, qquart)], qx, xpart)
    value = flat[pl.ds(at3, bit), :]
    for o in range(1, depth):
        mail.take(("r3", o), got3.at[o - 1], zparts[o])
        value = value + got3[o - 1]
    rows[pl.ds(at3, bit), :] = value
    here = rows.at[pl.ds(at3, bit)]
    for o in range(1, depth):
        mail.start(("r4", o), here, here, zparts[o])
    mail.take("q2", qx, xpart)
    qs[pl.ds(qat, qquart), :] = qs[pl.ds(qat, qquart), :] + qx[...]
    for o in range(1, depth):
        mail.start(("q3", o), qs.at[pl.ds(qat, qquart)], qz.at[o - 1], zparts[o])
    for o in range(1, depth):
        mail.take(("r4", o), rows.at[pl.ds(at2 + ((z + depth - o) % depth) * bit, bit)], zparts[o])
    here = rows.at[pl.ds(at2, quarter)]
    mail.start("r5", here, here, xpart)
    value = qs[pl.ds(qat, qquart), :]
    for o in range(1, depth):
        mail.take(("q3", o), qz.at[o - 1], zparts[o])
        value = value + qz[o - 1]
    qrow = grp * qpart
    q[pl.ds(qrow + qat, qquart), :] = value
    here = q.at[pl.ds(qrow + qat, qquart)]
    mail.start("q4", here, here, xpart)
    mail.take("r5", rows.at[pl.ds(at1 + (1 - xhi) * quarter, quarter)], xpart)
    here = rows.at[pl.ds(at1, half)]
    mail.start("r6", here, here, cpart)
    mail.take("q4", q.at[pl.ds(qrow + core * qhalf + (1 - xhi) * qquart, qquart)], xpart)
    here = q.at[pl.ds(qrow + core * qhalf, qhalf)]
    mail.start("q5", here, here, cpart)
    mail.take("r6", rows.at[pl.ds((1 - core) * half, half)], cpart)

    for c in range(size // LANES):
        picked[:, c * LANES : (c + 1) * LANES] = rows[pl.ds(c * width, width), :]
    loads["inverse"].wait()
    project[...] = dot(minv[...], picked[...], 1, 1).astype(BF16)
    scenario = asg[grp]
    weight = 0.0
    for i in range(groups):
        weight = weight + jnp.where(scenario == i, prob[i], 0.0)
    corner[...] = weight * dot(picked[...], project[...], 1, 0)
    cpiece = width // groups
    for o in near:
        mail.start(("c1", o), corner.at[pl.ds((grp ^ o) * cpiece, cpiece)], corner_got.at[o], peer[o])
    mail.take("q5", q.at[pl.ds(qrow + (1 - core) * qhalf, qhalf)], cpart)
    here = q.at[pl.ds(qrow, qpart)]
    for o in near:
        mail.start(("q6", o), here, here, peer[o])

    ra, rb = split(own, 0.6)

    def block(o):
        return weight * jnp.dot(big[o], project[...], preferred_element_type=F32)

    def make(y):
        side = block(2 * y + 1)
        encode(side[ra:], xb.at[y], xb_s.at[y])
        if y:
            encode(side[:ra], ya.at[y, 1], ya_s.at[y, 1])
            same = block(2 * y)
            encode(same[:ra], ya.at[y, 0], ya_s.at[y, 0])
            keep_b[y] = same[ra:]
        else:
            keep_a[...] = side[:ra]

    def ship(y):
        mail.start(("xbs", y), xb_s.at[y], xb_sg.at[y], peer[1])
        mail.start(("xb", y), xb.at[y], xb_g.at[y], peer[1])
        if y:
            mail.start(("yas", y), ya_s.at[y], ya_sg.at[y], peer[2 * y])
            mail.start(("ya", y), ya.at[y], ya_g.at[y], peer[2 * y])

    early = ys[:2]
    for y in early:
        make(y)
    value = corner[pl.ds(grp * cpiece, cpiece), :]
    for o in near:
        mail.take(("c1", o), corner_got.at[o], peer[o])
        value = value + corner_got[o]
    corner_sum[pl.ds(grp * cpiece, cpiece), :] = value
    here = corner_sum.at[pl.ds(grp * cpiece, cpiece)]
    for o in near:
        mail.start(("c2", o), here, here, peer[o])
    for y in early:
        ship(y)
    for y in ys[2:] + [0]:
        make(y)
        ship(y)
    for o in near:
        mail.take(("q6", o), q.at[pl.ds((grp ^ o) * qpart, qpart)], peer[o])
    picks = jnp.concatenate([q[pl.ds(c * width, width), :] for c in range(2)], axis=1)
    keep0[...] = block(0) - dot(prior[...], picks, 1, 1)
    less = dot(picks, picks, 1, 1)
    for o in near:
        mail.take(("c2", o), corner_sum.at[pl.ds((grp ^ o) * cpiece, cpiece)], peer[o])
    a = corner_sum[...] - less
    a = 0.5 * (a + jnp.transpose(a))

    def onward(y):
        mail.take(("xbs", y), xb_sg.at[y], peer[1])
        mail.take(("xb", y), xb_g.at[y], peer[1])
        encode(keep_b[y] + decode(xb_g[y], xb_sg[y]), yb.at[y], yb_s.at[y])
        mail.start(("ybs", y), yb_s.at[y], yb_sg.at[y], peer[2 * y])
        mail.start(("yb", y), yb.at[y], yb_g.at[y], peer[2 * y])

    def across():
        value, here = keep_a[...], keep0[:ra, :]
        for y in ys:
            mail.take(("yas", y), ya_sg.at[y], peer[2 * y])
            mail.take(("ya", y), ya_g.at[y], peer[2 * y])
            value = value + decode(ya_g[y, 1], ya_sg[y, 1])
            here = here + decode(ya_g[y, 0], ya_sg[y, 0])
        encode(value, xa, xa_s)
        mail.start("xas", xa_s, xa_sg, peer[1])
        mail.start("xa", xa, xa_g, peer[1])
        keep0[:ra, :] = here

    steps = [functools.partial(onward, y) for y in ys[:2]]
    hooks = [lambda: [f() for f in steps[:1]], lambda: [f() for f in steps[1:] + [across]], lambda: [onward(y) for y in ys[2:]]]
    w = inverse_factor(a, work, invb, hooks)

    mail.take("xas", xa_sg, peer[1])
    mail.take("xa", xa_g, peer[1])
    mail.take(("xbs", 0), xb_sg.at[0], peer[1])
    mail.take(("xb", 0), xb_g.at[0], peer[1])
    upper = keep0[:ra, :] + decode(xa_g[...], xa_sg[...])
    lower = keep0[ra:, :] + decode(xb_g[0], xb_sg[0])
    for y in ys:
        mail.take(("ybs", y), yb_sg.at[y], peer[2 * y])
        mail.take(("yb", y), yb_g.at[y], peer[2 * y])
        lower = lower + decode(yb_g[y], yb_sg[y])
    solved = dot(jnp.concatenate([upper, lower], axis=0), w, 1, 1, HIGHEST)
    solved = jnp.where(hit[...] > 0.5, 0.0, solved)
    panel[...] = solved
    pan[0] = solved.astype(BF16)

    pa, pb = split(own, 0.4)
    top, low = pl.ds(0, pa), pl.ds(pa, pb)
    mail.start("g1", pan.at[0, low], pan.at[1, low], peer[1])
    for y in ys:
        mail.start(("g2", y), pan.at[0, top], pan.at[2 * y, top], peer[2 * y])
    mail.start("g3", pan.at[0, top], pan.at[1, top], peer[1])
    for y in ys:
        mail.start(("g4", y), pan.at[0, low], pan.at[2 * y, low], peer[2 * y])
    acc[...] = dot(pan[0], big[0], 0, 0)
    mail.take("g1", pan.at[1, low], peer[1])
    for y in ys:
        mail.start(("g5", y), pan.at[1, low], pan.at[2 * y + 1, low], peer[2 * y])
    for y in ys[1:] + ys[:1]:
        mail.take(("g2", y), pan.at[2 * y, top], peer[2 * y])
        mail.start(("g6", y), pan.at[2 * y, top], pan.at[2 * y + 1, top], peer[1])
    mail.take("g3", pan.at[1, top], peer[1])
    acc[...] += dot(pan[1], big[1], 0, 0)
    for y in ys[1:] + ys[:1]:
        mail.take(("g4", y), pan.at[2 * y, low], peer[2 * y])
        acc[...] += dot(pan[2 * y], big[2 * y], 0, 0)
    for y in ys[1:] + ys[:1]:
        mail.take(("g5", y), pan.at[2 * y + 1, low], peer[2 * y])
        mail.take(("g6", y), pan.at[2 * y + 1, top], peer[1])
        acc[...] += dot(pan[2 * y + 1], big[2 * y + 1], 0, 0)

    piece = sums.shape[3]
    scale = 1.0 / math.sqrt(N1)
    for e in range(acc.shape[1] // LANES):
        turned = jnp.transpose(acc[:, e * LANES : (e + 1) * LANES]) * scale
        for k in range(LANES // piece):
            n = e * (LANES // piece) + k
            zz, xx, cc = n // (XHI * CORES), (n // CORES) % XHI, n % CORES
            sums[cc, xx, zz] = turned[k * piece : (k + 1) * piece, :]
    mail.start("s1", sums.at[1 - core], core_got, cpart)
    mail.take("s1", core_got, cpart)
    keep1[...] = (sums[core] + core_got[...]).reshape(keep1.shape)
    encode(keep1[1 - xhi], x_code, x_scale)
    mail.start("s2s", x_scale, x_sgot, xpart)
    mail.start("s2", x_code, x_got, xpart)
    mail.take("s2s", x_sgot, xpart)
    mail.take("s2", x_got, xpart)
    value = keep1[xhi] + decode(x_got[...], x_sgot[...])
    keep2[...] = value.reshape(keep2.shape)
    peak = jnp.maximum(jnp.max(jnp.abs(value), axis=0, keepdims=True), 1e-30)
    z_scale[...] = peak * (1.0 / TOP)
    z_code[...] = jnp.round(value * (TOP / peak)).astype(jnp.int32).astype(I16).reshape(z_code.shape)
    for o in range(1, depth):
        mail.start(("s3s", o), z_scale, z_sgot.at[o - 1], zparts[o])
        mail.start(("s3", o), z_code.at[(z + o) % depth], z_got.at[o - 1], zparts[o])
    value = keep2[z]
    for o in range(1, depth):
        mail.take(("s3s", o), z_sgot.at[o - 1], zparts[o])
        mail.take(("s3", o), z_got.at[o - 1], zparts[o])
        value = value + decode(z_got[o - 1], z_sgot[o - 1])
    out[...] = value
    mail.close()
    assert len(mail.ids) <= send.shape[0], len(mail.ids)


def call(groups, count, border, inverse, prior, sel, asg, prob):
    size = border.shape[1]
    own, width = prior.shape
    depth = count // (CORES * XHI)
    n = max(depth - 1, 1)
    piece = size // count
    high = size // LANES * width
    qpart = 2 * width // groups
    ny = groups // XLO
    ra, rb = split(own, 0.6)
    dma, vmem = pltpu.SemaphoreType.DMA, pltpu.VMEM
    vm = pl.BlockSpec(memory_space=vmem)
    anyspace = pl.BlockSpec(memory_space=pl.ANY)
    sm = pl.BlockSpec(memory_space=pltpu.SMEM)
    return pl.pallas_call(
        functools.partial(kernel, groups, count),
        out_shape=(jax.ShapeDtypeStruct((own, width), F32), jax.ShapeDtypeStruct((piece, width), F32)),
        in_specs=[anyspace, anyspace, anyspace, vm, sm, sm],
        out_specs=(vm, vm),
        scratch_shapes=[
            vmem((groups, own, size), BF16),
            vmem((size, size), BF16),
            vmem((own, width), BF16),
            vmem((high, LANES), BF16),
            vmem((high, LANES), BF16),
            vmem((high // CORES, LANES), BF16),
            vmem((high // (CORES * XHI), LANES), BF16),
            vmem((n, high // count, LANES), BF16),
            vmem((2 * width, LANES), BF16),
            vmem((groups, qpart, LANES), BF16),
            vmem((qpart, LANES), BF16),
            vmem((qpart // CORES, LANES), BF16),
            vmem((qpart // (CORES * XHI), LANES), BF16),
            vmem((n, qpart // (CORES * XHI), LANES), BF16),
            vmem((2 * width, LANES), BF16),
            vmem((width, size), BF16),
            vmem((size, width), BF16),
            vmem((width, width), F32),
            vmem((groups, width // groups, width), F32),
            vmem((width, width), F32),
            vmem((ny, 2, ra, width), I16),
            vmem((ny, 2, 1, width), F32),
            vmem((ny, 2, ra, width), I16),
            vmem((ny, 2, 1, width), F32),
            vmem((ny, rb, width), I16),
            vmem((ny, 1, width), F32),
            vmem((ny, rb, width), I16),
            vmem((ny, 1, width), F32),
            vmem((ra, width), I16),
            vmem((1, width), F32),
            vmem((ra, width), I16),
            vmem((1, width), F32),
            vmem((ny, rb, width), I16),
            vmem((ny, 1, width), F32),
            vmem((ny, rb, width), I16),
            vmem((ny, 1, width), F32),
            vmem((own, width), F32),
            vmem((ra, width), F32),
            vmem((ny, rb, width), F32),
            vmem((own, width), F32),
            vmem((BASE, 2 * BASE), F32),
            vmem((BASE, BASE), F32),
            vmem((groups, own, width), BF16),
            vmem((width, size), F32),
            vmem((CORES, XHI, depth, piece, width), F32),
            vmem((XHI, depth, piece, width), F32),
            vmem((XHI, depth * piece, width), F32),
            vmem((depth * piece, width), I16),
            vmem((1, width), F32),
            vmem((depth * piece, width), I16),
            vmem((1, width), F32),
            vmem((depth, piece, width), F32),
            vmem((depth, piece, width), I16),
            vmem((1, width), F32),
            vmem((n, piece, width), I16),
            vmem((n, 1, width), F32),
            dma((groups + 2,)),
            dma((128,)),
            dma((128,)),
        ],
        compiler_params=pltpu.CompilerParams(
            collective_id=0, has_side_effects=True, vmem_limit_bytes=60 << 20
        ),
        name="panel",
    )(border, inverse, prior, sel, asg, prob)


def body(border, inverse_blocks, selected, assignment, probability, prior_panel):
    groups, count = lax.axis_size("grp"), lax.axis_size("dev")
    panel, residual = call(
        groups, count, border[0], inverse_blocks[0], prior_panel, selected[None, :], assignment, probability
    )
    return (panel, residual[None])


def solution(mesh):
    return jax.shard_map(
        body,
        mesh=mesh,
        in_specs=(
            P("grp", "dev", None),
            P("grp", None, None),
            P(),
            P(),
            P(),
            P(("dev", "grp"), None),
        ),
        out_specs=(P(("dev", "grp"), None), P("grp", "dev", None)),
        check_vma=False,
    )
```

```python
import functools
import math

import jax
import jax.numpy as jnp
from jax import lax
from jax.experimental import pallas as pl
from jax.experimental.pallas import tpu as pltpu
from jax.sharding import PartitionSpec as P

N1 = 131072
MESH = pl.DeviceIdType.MESH
HIGHEST = lax.Precision.HIGHEST
F32 = jnp.float32
BF16 = jnp.bfloat16
I16 = jnp.int16
LANES = 128
CORES, XHI, XLO = 2, 2, 2
TOP = 32767.0
BASE, PANEL = 128, 16


def dot(a, b, ca, cb, precision=None):
    return lax.dot_general(
        a, b, (((ca,), (cb,)), ((), ())), precision=precision, preferred_element_type=F32
    )


def split(own, share):
    part = max(16, int(own * share / 16 + 0.5) * 16)
    return own - part, part


def encode(x, code, scale):
    peak = jnp.maximum(jnp.max(jnp.abs(x), axis=0, keepdims=True), 1e-30)
    code[...] = jnp.round(x * (TOP / peak)).astype(jnp.int32).astype(I16)
    scale[...] = peak * (1.0 / TOP)


def decode(code, scale):
    return code.astype(jnp.int32).astype(F32) * scale


def eliminate(work, inv, hooks):
    size = work.shape[0]
    shape = (PANEL, size)
    row = lax.broadcasted_iota(jnp.int32, shape, 0)
    spread = lambda x: jnp.broadcast_to(x, shape)
    left, right = slice(0, size), slice(size, 2 * size)
    for at in range(0, size, PANEL):
        here = slice(at, at + PANEL)
        block, side = work[here, left], work[here, right]
        cs = [spread(block[:, at + j : at + j + 1]) for j in range(PANEL)]
        pivots = jnp.zeros(shape, F32)
        for j in range(PANEL):
            pivots = jnp.where(row == j, cs[j], pivots)
            m = jnp.where(row > j, cs[j] * spread(1.0 / cs[j][j : j + 1, :]), 0.0)
            for k in range(j + 1, PANEL):
                cs[k] = cs[k] - m * spread(cs[k][j : j + 1, :])
            block = block - m * spread(block[j : j + 1, :])
            side = side - m * spread(side[j : j + 1, :])
        r = lax.rsqrt(pivots)
        r = r * (1.5 - 0.5 * pivots * r * r)
        block, side = block * r, side * r
        inv[here, :] = side
        turned = jnp.transpose(block)
        for to in range(at + PANEL, size, PANEL):
            there = slice(to, to + PANEL)
            a, b = work[there, left], work[there, right]
            for j in range(PANEL):
                t = spread(turned[there, j : j + 1])
                a = a - t * spread(block[j : j + 1, :])
                b = b - t * spread(side[j : j + 1, :])
            work[there, left] = a
            work[there, right] = b
        hooks.pop(0)()


def inverse_factor(a, work, inv, hooks):
    n = a.shape[0]
    if n == BASE:
        i = lax.broadcasted_iota(jnp.int32, (n, n), 0)
        j = lax.broadcasted_iota(jnp.int32, (n, n), 1)
        work[...] = jnp.concatenate([a, (i == j).astype(F32)], axis=1)
        eliminate(work, inv, hooks)
        return inv[...]
    h = n // 2
    w11 = inverse_factor(a[:h, :h], work, inv, hooks)
    l21 = dot(a[h:, :h], w11, 1, 1, HIGHEST)
    w22 = inverse_factor(a[h:, h:] - dot(l21, l21, 1, 1, HIGHEST), work, inv, hooks)
    w21 = -dot(dot(w22, l21, 1, 0, HIGHEST), w11, 1, 0, HIGHEST)
    top = jnp.concatenate([w11, jnp.zeros((h, h), F32)], axis=1)
    return jnp.concatenate([top, jnp.concatenate([w21, w22], axis=1)], axis=0)


class Mail:
    def __init__(self, send, recv):
        self.send, self.recv, self.ids, self.started = send, recv, {}, {}

    def copy(self, key, src, dst, where):
        k = self.ids.setdefault(key, len(self.ids))
        return pltpu.make_async_remote_copy(
            src_ref=src, dst_ref=dst, send_sem=self.send.at[k], recv_sem=self.recv.at[k],
            device_id=where, device_id_type=MESH,
        )

    def start(self, key, src, dst, where, whole=None):
        self.copy(key, src() if callable(src) else src, dst, where).start()
        assert whole is not None or key not in self.started, key
        self.started[key] = (src if whole is None else whole, where)

    def take(self, key, dst, where):
        self.copy(key, dst, dst, where).wait_recv()

    def close(self):
        for key, (ref, where) in self.started.items():
            ref = ref() if callable(ref) else ref
            self.copy(key, ref, ref, where).wait_send()


def kernel(
    groups, count, border, inverse, prior_hbm, sel, asg, prob, panel, out,
    big, minv, prior, flat, rows, got1, got2, q0, qh, qx, qz, qv, qg, q, picked, project,
    corner, corner_got, corner_sum, ya, ya_s, ya_g, ya_sg, xb, xb_s, xb_g, xb_sg,
    xa, xa_s, xa_g, xa_sg, yb, yb_s, yb_g, yb_sg, keep0, keep_a, keep_b, hit, work, invb,
    pan, acc, sums, core_got, keep1, z_code, z_scale, z_got, z_sgot,
    load, send, recv,
):
    grp, dev = lax.axis_index("grp"), lax.axis_index("dev")
    depth = count // (CORES * XHI)
    z, xhi, core = dev // (CORES * XHI), (dev // CORES) % XHI, dev % CORES
    at = lambda zz, xx, cc: (grp, (zz * XHI + xx) * CORES + cc)
    cpart, xpart = at(z, xhi, 1 - core), at(z, 1 - xhi, core)
    zparts = {o: at((z + o) % depth, xhi, core) for o in range(1, depth)}
    far = sorted(range(depth), key=lambda o: -min(o, depth - o))
    chips = [(o, x) for o in far for x in (1, 0) if (o, x) != (0, 0)]
    chip = {c: at((z + c[0]) % depth, xhi ^ c[1], core) for c in chips}
    slot = {c: i for i, c in enumerate(chips)}
    ys = [y for y in (2, 1, 3) if y < groups // XLO]
    near = [o for o in (5, 4, 7, 6, 3, 2, 1) if o < groups]
    peer = {o: (grp ^ o, dev) for o in near}
    width, size = picked.shape
    own = prior.shape[0]
    mail = Mail(send, recv)

    def fenced(f, *args):
        pl.when(grp >= 0)(functools.partial(f, *args))

    loads = {o: pltpu.make_async_copy(border.at[pl.ds((grp ^ o) * own, own)], big.at[o], load.at[o]) for o in range(groups)}
    loads["prior"] = pltpu.make_async_copy(prior_hbm, prior, load.at[groups])
    loads["inverse"] = pltpu.make_async_copy(inverse, minv, load.at[groups + 1])
    for name in ["prior"] + list(range(groups)) + ["inverse"]:
        loads[name].start()
    barrier = pltpu.get_barrier_semaphore()
    partners = [cpart] + list(chip.values()) + list(peer.values())
    for where in partners:
        pl.semaphore_signal(barrier, inc=1, device_id=where, device_id_type=MESH)

    want = jnp.transpose(jnp.broadcast_to(sel[...], (LANES, width)))[:, :1]
    want = jnp.broadcast_to(want, (width, own))
    lanes = lax.broadcasted_iota(jnp.int32, (width, own), 1)
    first = (dev * groups + grp) * own
    loads["prior"].wait()
    mine = dot((want - first == lanes).astype(F32).astype(BF16), prior[...], 1, 0).astype(BF16)
    for c in range(2):
        q0[pl.ds(c * width, width), :] = mine[:, c * LANES : (c + 1) * LANES]
    total = None
    for o in range(groups):
        loads[o].wait()
        base = (dev * groups + (grp ^ o)) * own
        part = dot((want - base == lanes).astype(F32).astype(BF16), big[o], 1, 0)
        total = part if total is None else total + part
    total = total.astype(BF16)
    for c in range(size // LANES):
        flat[pl.ds(c * width, width), :] = total[:, c * LANES : (c + 1) * LANES]
    pl.semaphore_wait(barrier, len(partners))

    high = flat.shape[0]
    half, quarter, bit = high // CORES, high // (CORES * XHI), high // count
    qhalf, qquart, qbit = 2 * width // CORES, 2 * width // (CORES * XHI), 2 * width // count
    at1 = core * half
    at3 = at1 + xhi * quarter + z * bit
    qat1 = core * qhalf
    qat2 = qat1 + xhi * qquart
    qat3 = qat2 + z * qbit
    mail.start("r1", flat.at[pl.ds((1 - core) * half, half)], got1, cpart)
    mail.start("q1", q0.at[pl.ds((1 - core) * qhalf, qhalf)], qh, cpart)
    mail.take("r1", got1, cpart)
    flat[pl.ds(at1, half), :] = flat[pl.ds(at1, half), :] + got1[...]
    for c in chips:
        there = at1 + (xhi ^ c[1]) * quarter + ((z + c[0]) % depth) * bit
        mail.start("r2", flat.at[pl.ds(there, bit)], got2.at[slot[c]], chip[c], got2)
    mail.take("q1", qh, cpart)
    q0[pl.ds(qat1, qhalf), :] = q0[pl.ds(qat1, qhalf), :] + qh[...]
    mail.start("q2", q0.at[pl.ds(qat1 + (1 - xhi) * qquart, qquart)], qx, xpart)
    ids = first + lax.broadcasted_iota(jnp.int32, (own, width), 0)
    marked = jnp.max((ids == sel[...]).astype(F32), axis=1, keepdims=True)
    hit[...] = jnp.broadcast_to(marked, hit.shape)
    mail.take("q2", qx, xpart)
    q0[pl.ds(qat2, qquart), :] = q0[pl.ds(qat2, qquart), :] + qx[...]
    for o in zparts:
        mail.start("q3", q0.at[pl.ds(qat2 + ((z + o) % depth) * qbit, qbit)], qz.at[o - 1], zparts[o], qz)
    mail.take("r2", got2, xpart)
    value = flat[pl.ds(at3, bit), :]
    for c in chips:
        value = value + got2[slot[c]]
    rows[pl.ds(at3, bit), :] = value
    here = rows.at[pl.ds(at3, bit)]
    rings = [chips[i : i + 5] for i in range(0, len(chips), 5)]
    for n, ring in enumerate(rings):
        for c in ring:
            mail.start(("r3", n), here, here, chip[c], got2.at[pl.ds(0, len(ring))])
    other = rows.at[pl.ds((1 - core) * half, half)]
    mail.start("r4", here, here, cpart, other)
    value = q0[pl.ds(qat3, qbit), :]
    if zparts:
        mail.take("q3", qz, xpart)
    for o in zparts:
        value = value + qz[o - 1]
    qv[...] = value
    for n, o in enumerate(near):
        mail.start("q4", qv, qg.at[n], peer[o], qg)

    def forward(n):
        mail.take(("r3", n), got2.at[pl.ds(0, len(rings[n]))], xpart)
        for c in rings[n]:
            there = rows.at[pl.ds(at1 + (xhi ^ c[1]) * quarter + ((z + depth - c[0]) % depth) * bit, bit)]
            mail.start("r4", there, there, cpart, other)

    order = list(range(len(rings)))[::-1]
    forward(order[0])
    mail.take("q4", qg, xpart)
    value = qv[...]
    for n in range(len(near)):
        value = value + qg[n]
    q[pl.ds(qat3, qbit), :] = value
    here = q.at[pl.ds(qat3, qbit)]
    mail.start("q5", here, here, xpart)
    for n in order[1:]:
        forward(n)
    mail.take("r4", other, cpart)

    for c in range(size // LANES):
        picked[:, c * LANES : (c + 1) * LANES] = rows[pl.ds(c * width, width), :]
    loads["inverse"].wait()
    project[...] = dot(minv[...], picked[...], 1, 1).astype(BF16)
    scenario = asg[grp]
    weight = 0.0
    for i in range(groups):
        weight = weight + jnp.where(scenario == i, prob[i], 0.0)
    corner[...] = weight * dot(picked[...], project[...], 1, 0)
    chalf, cpiece = width // CORES, width // CORES // depth
    cmine = pl.ds(core * chalf + z * cpiece, cpiece)
    for n, o in enumerate(near):
        mail.start("c1", corner.at[cmine], corner_got.at[n], peer[o], corner_got)
    ra, rb = split(own, 0.5)

    def block(o):
        return weight * jnp.dot(big[o], project[...], preferred_element_type=F32)

    def make(y):
        side = block(2 * y + 1)
        encode(side[ra:], xb.at[y], xb_s.at[y])
        if y:
            encode(side[:ra], ya.at[y, 1], ya_s.at[y, 1])
            same = block(2 * y)
            encode(same[:ra], ya.at[y, 0], ya_s.at[y, 0])
            keep_b[y] = same[ra:]
        else:
            keep_a[...] = side[:ra]

    def ship(y):
        mail.start(("xbs", y), lambda: xb_s.at[y], xb_sg.at[y], peer[1])
        mail.start(("xb", y), lambda: xb.at[y], xb_g.at[y], peer[1])
        if y:
            mail.start(("yas", y), lambda: ya_s.at[y], ya_sg.at[y], peer[2 * y])
            mail.start(("ya", y), lambda: ya.at[y], ya_g.at[y], peer[2 * y])

    lots = q.at[pl.ds(0, XHI * (depth - 1) * qbit)]
    rest = corner_sum.at[pl.ds(0, (depth - 1) * cpiece)]

    def blocks(y):
        make(y)
        ship(y)

    def corner_out():
        mail.take("c1", corner_got, xpart)
        value = corner[cmine, :]
        for n in range(len(near)):
            value = value + corner_got[n]
        corner_sum[cmine, :] = value
        here = corner_sum.at[cmine]
        for o in zparts:
            mail.start("c2", here, here, zparts[o], lambda: rest)

    def prior_out():
        mail.take("q5", q.at[pl.ds(qat1 + (1 - xhi) * qquart + z * qbit, qbit)], xpart)
        for o in zparts:
            for x in range(XHI):
                here = q.at[pl.ds(qat1 + x * qquart + z * qbit, qbit)]
                mail.start("q6", here, here, zparts[o], lambda: lots)

    def prior_over():
        if zparts:
            mail.take("q6", lots, xpart)
        here = lambda: q.at[pl.ds(qat1, qhalf)]
        mail.start("q7", here, here(), cpart)

    for y in ys[:1]:
        fenced(blocks, y)
    fenced(prior_out)
    for y in ys[1:2]:
        fenced(blocks, y)
    fenced(corner_out)
    for y in ys[2:] + [0]:
        fenced(blocks, y)
    fenced(prior_over)
    keep0[...] = block(0)
    mail.take("q7", q.at[pl.ds((1 - core) * qhalf, qhalf)], cpart)
    picks = jnp.concatenate([q[pl.ds(c * width, width), :] for c in range(2)], axis=1)
    keep0[...] -= dot(prior[...], picks, 1, 1)
    less = dot(picks, picks, 1, 1)
    if zparts:
        mail.take("c2", rest, xpart)
    here = corner_sum.at[pl.ds(core * chalf, chalf)]
    mail.start("c3", here, here, cpart)
    mail.take("c3", corner_sum.at[pl.ds((1 - core) * chalf, chalf)], cpart)
    a = corner_sum[...] - less
    a = 0.5 * (a + jnp.transpose(a))

    def onward(y):
        mail.take(("xbs", y), xb_sg.at[y], peer[1])
        mail.take(("xb", y), xb_g.at[y], peer[1])
        encode(keep_b[y] + decode(xb_g[y], xb_sg[y]), yb.at[y], yb_s.at[y])
        mail.start(("ybs", y), lambda: yb_s.at[y], yb_sg.at[y], peer[2 * y])
        mail.start(("yb", y), lambda: yb.at[y], yb_g.at[y], peer[2 * y])

    def across():
        value, here = keep_a[...], keep0[:ra, :]
        for y in ys:
            mail.take(("yas", y), ya_sg.at[y], peer[2 * y])
            mail.take(("ya", y), ya_g.at[y], peer[2 * y])
            value = value + decode(ya_g[y, 1], ya_sg[y, 1])
            here = here + decode(ya_g[y, 0], ya_sg[y, 0])
        encode(value, xa, xa_s)
        mail.start("xas", xa_s, xa_sg, peer[1])
        mail.start("xa", xa, xa_g, peer[1])
        keep0[:ra, :] = here

    hooks = [lambda: None for _ in range(width // PANEL)]
    for y, n in zip(ys, (0, 1, 4)):
        hooks[n] = functools.partial(fenced, onward, y)
    hooks[7] = functools.partial(fenced, across)
    w = inverse_factor(a, work, invb, hooks)

    mail.take("xas", xa_sg, peer[1])
    mail.take("xa", xa_g, peer[1])
    mail.take(("xbs", 0), xb_sg.at[0], peer[1])
    mail.take(("xb", 0), xb_g.at[0], peer[1])
    upper = keep0[:ra, :] + decode(xa_g[...], xa_sg[...])
    lower = keep0[ra:, :] + decode(xb_g[0], xb_sg[0])
    for y in ys:
        mail.take(("ybs", y), yb_sg.at[y], peer[2 * y])
        mail.take(("yb", y), yb_g.at[y], peer[2 * y])
        lower = lower + decode(yb_g[y], yb_sg[y])
    solved = dot(jnp.concatenate([upper, lower], axis=0), w, 1, 1, HIGHEST)
    solved = jnp.where(hit[...] > 0.5, 0.0, solved)
    panel[...] = solved
    pan[0] = solved.astype(BF16)

    pa, pb = split(own, 0.4)
    top, low = pl.ds(0, pa), pl.ds(pa, pb)
    mail.start("g1", pan.at[0, low], pan.at[1, low], peer[1])
    for y in ys:
        mail.start(("g2", y), pan.at[0, top], pan.at[2 * y, top], peer[2 * y])
    mail.start("g3", pan.at[0, top], pan.at[1, top], peer[1])
    for y in ys:
        mail.start(("g4", y), pan.at[0, low], pan.at[2 * y, low], peer[2 * y])
    acc[...] = dot(pan[0], big[0], 0, 0)
    mail.take("g1", pan.at[1, low], peer[1])
    for y in ys:
        mail.start(("g5", y), pan.at[1, low], pan.at[2 * y + 1, low], peer[2 * y])
    for y in ys[1:] + ys[:1]:
        mail.take(("g2", y), pan.at[2 * y, top], peer[2 * y])
        mail.start(("g6", y), pan.at[2 * y, top], pan.at[2 * y + 1, top], peer[1])
    mail.take("g3", pan.at[1, top], peer[1])
    acc[...] += dot(pan[1], big[1], 0, 0)
    for y in ys[1:] + ys[:1]:
        mail.take(("g4", y), pan.at[2 * y, low], peer[2 * y])
        acc[...] += dot(pan[2 * y], big[2 * y], 0, 0)
    for y in ys[1:] + ys[:1]:
        mail.take(("g5", y), pan.at[2 * y + 1, low], peer[2 * y])
        mail.take(("g6", y), pan.at[2 * y + 1, top], peer[1])
        acc[...] += dot(pan[2 * y + 1], big[2 * y + 1], 0, 0)

    piece = sums.shape[3]
    scale = 1.0 / math.sqrt(N1)
    halves = [range(0, (depth + 1) // 2), range((depth + 1) // 2, depth)]
    halves = [h for h in halves if len(h)]
    tiles = acc.shape[1] // LANES
    done = 0
    for e in range(tiles):
        turned = jnp.transpose(acc[:, e * LANES : (e + 1) * LANES]) * scale
        for k in range(LANES // piece):
            n = e * (LANES // piece) + k
            zz, xx, cc = n // (XHI * CORES), (n // CORES) % XHI, n % CORES
            sums[cc, zz, xx] = turned[k * piece : (k + 1) * piece, :]
        if done < len(halves) and n + 1 == len(halves[done]) * XHI * CORES + (halves[done][0]) * XHI * CORES:
            part = pl.ds(halves[done][0], len(halves[done]))
            mail.start(("s1", done), sums.at[1 - core, part], core_got.at[part], cpart)
            done += 1
    assert done == len(halves)
    for n, h in enumerate(halves):
        mail.take(("s1", n), core_got.at[pl.ds(h[0], len(h))], cpart)
    value = (sums[core] + core_got[...]).reshape(depth * XHI * piece, width)
    keep1[...] = value.reshape(keep1.shape)
    peak = jnp.maximum(jnp.max(jnp.abs(value), axis=0, keepdims=True), 1e-30)
    z_scale[...] = peak * (1.0 / TOP)
    z_code[...] = jnp.round(value * (TOP / peak)).astype(jnp.int32).astype(I16).reshape(z_code.shape)
    for c in chips:
        mail.start("s2s", z_scale, z_sgot.at[slot[c]], chip[c], z_sgot)
        mail.start("s2", z_code.at[(z + c[0]) % depth, xhi ^ c[1]], z_got.at[slot[c]], chip[c], z_got)
    mail.take("s2s", z_sgot, xpart)
    mail.take("s2", z_got, xpart)
    value = keep1[z, xhi]
    for n in range(len(chips)):
        value = value + decode(z_got[n], z_sgot[n])
    out[...] = value
    mail.close()
    assert len(mail.ids) <= send.shape[0], len(mail.ids)


def call(groups, count, border, inverse, prior, sel, asg, prob):
    size = border.shape[1]
    own, width = prior.shape
    depth = count // (CORES * XHI)
    messages = 56
    n = max(depth - 1, 1)
    others = depth * XHI - 1
    piece = size // count
    high = size // LANES * width
    ny = groups // XLO
    ra, rb = split(own, 0.5)
    dma, vmem = pltpu.SemaphoreType.DMA, pltpu.VMEM
    vm = pl.BlockSpec(memory_space=vmem)
    anyspace = pl.BlockSpec(memory_space=pl.ANY)
    sm = pl.BlockSpec(memory_space=pltpu.SMEM)
    return pl.pallas_call(
        functools.partial(kernel, groups, count),
        out_shape=(jax.ShapeDtypeStruct((own, width), F32), jax.ShapeDtypeStruct((piece, width), F32)),
        in_specs=[anyspace, anyspace, anyspace, vm, sm, sm],
        out_specs=(vm, vm),
        scratch_shapes=[
            vmem((groups, own, size), BF16),
            vmem((size, size), BF16),
            vmem((own, width), BF16),
            vmem((high, LANES), BF16),
            vmem((high, LANES), BF16),
            vmem((high // CORES, LANES), BF16),
            vmem((others, high // count, LANES), BF16),
            vmem((2 * width, LANES), BF16),
            vmem((2 * width // CORES, LANES), BF16),
            vmem((2 * width // (CORES * XHI), LANES), BF16),
            vmem((n, 2 * width // count, LANES), BF16),
            vmem((2 * width // count, LANES), BF16),
            vmem((groups - 1, 2 * width // count, LANES), BF16),
            vmem((2 * width, LANES), BF16),
            vmem((width, size), BF16),
            vmem((size, width), BF16),
            vmem((width, width), F32),
            vmem((groups - 1, width // CORES // depth, width), F32),
            vmem((width, width), F32),
            vmem((ny, 2, ra, width), I16),
            vmem((ny, 2, 1, width), F32),
            vmem((ny, 2, ra, width), I16),
            vmem((ny, 2, 1, width), F32),
            vmem((ny, rb, width), I16),
            vmem((ny, 1, width), F32),
            vmem((ny, rb, width), I16),
            vmem((ny, 1, width), F32),
            vmem((ra, width), I16),
            vmem((1, width), F32),
            vmem((ra, width), I16),
            vmem((1, width), F32),
            vmem((ny, rb, width), I16),
            vmem((ny, 1, width), F32),
            vmem((ny, rb, width), I16),
            vmem((ny, 1, width), F32),
            vmem((own, width), F32),
            vmem((ra, width), F32),
            vmem((ny, rb, width), F32),
            vmem((own, width), F32),
            vmem((BASE, 2 * BASE), F32),
            vmem((BASE, BASE), F32),
            vmem((groups, own, width), BF16),
            vmem((width, size), F32),
            vmem((CORES, depth, XHI, piece, width), F32),
            vmem((depth, XHI, piece, width), F32),
            vmem((depth, XHI, piece, width), F32),
            vmem((depth, XHI, piece, width), I16),
            vmem((1, width), F32),
            vmem((others, piece, width), I16),
            vmem((others, 1, width), F32),
            dma((groups + 2,)),
            dma((messages,)),
            dma((messages,)),
        ],
        compiler_params=pltpu.CompilerParams(
            collective_id=0, has_side_effects=True, vmem_limit_bytes=60 << 20
        ),
        name="panel",
    )(border, inverse, prior, sel, asg, prob)


def body(border, inverse_blocks, selected, assignment, probability, prior_panel):
    groups, count = lax.axis_size("grp"), lax.axis_size("dev")
    panel, residual = call(
        groups, count, border[0], inverse_blocks[0], prior_panel, selected[None, :], assignment, probability
    )
    return (panel, residual[None])


def solution(mesh):
    return jax.shard_map(
        body,
        mesh=mesh,
        in_specs=(
            P("grp", "dev", None),
            P("grp", None, None),
            P(),
            P(),
            P(),
            P(("dev", "grp"), None),
        ),
        out_specs=(P(("dev", "grp"), None), P("grp", "dev", None)),
        check_vma=False,
    )
```

```python
import functools
import math

import jax
import jax.numpy as jnp
from jax import lax
from jax.experimental import pallas as pl
from jax.experimental.pallas import tpu as pltpu
from jax.sharding import PartitionSpec as P

N1 = 131072
MESH = pl.DeviceIdType.MESH
HIGHEST = lax.Precision.HIGHEST
F32 = jnp.float32
BF16 = jnp.bfloat16
I16 = jnp.int16
LANES = 128
CORES, XHI, XLO = 2, 2, 2
TOP = 32767.0
BASE, PANEL = 128, 16


def dot(a, b, ca, cb, precision=None):
    return lax.dot_general(
        a, b, (((ca,), (cb,)), ((), ())), precision=precision, preferred_element_type=F32
    )


def split(own, share):
    part = max(16, int(own * share / 16 + 0.5) * 16)
    return own - part, part


def encode(x, code, scale):
    peak = jnp.maximum(jnp.max(jnp.abs(x), axis=0, keepdims=True), 1e-30)
    code[...] = jnp.round(x * (TOP / peak)).astype(jnp.int32).astype(I16)
    scale[...] = peak * (1.0 / TOP)


def decode(code, scale):
    return code.astype(jnp.int32).astype(F32) * scale


def eliminate(work, inv, hooks):
    size = work.shape[0]
    shape = (PANEL, size)
    row = lax.broadcasted_iota(jnp.int32, shape, 0)
    spread = lambda x: jnp.broadcast_to(x, shape)
    left, right = slice(0, size), slice(size, 2 * size)
    for at in range(0, size, PANEL):
        here = slice(at, at + PANEL)
        block, side = work[here, left], work[here, right]
        cs = [spread(block[:, at + j : at + j + 1]) for j in range(PANEL)]
        pivots = jnp.zeros(shape, F32)
        for j in range(PANEL):
            pivots = jnp.where(row == j, cs[j], pivots)
            m = jnp.where(row > j, cs[j] * spread(1.0 / cs[j][j : j + 1, :]), 0.0)
            for k in range(j + 1, PANEL):
                cs[k] = cs[k] - m * spread(cs[k][j : j + 1, :])
            block = block - m * spread(block[j : j + 1, :])
            side = side - m * spread(side[j : j + 1, :])
        r = lax.rsqrt(pivots)
        r = r * (1.5 - 0.5 * pivots * r * r)
        block, side = block * r, side * r
        inv[here, :] = side
        turned = jnp.transpose(block)
        if at + PANEL < size:
            there = slice(at + PANEL, at + 2 * PANEL)
            a, b = work[there, left], work[there, right]
            for j in range(PANEL):
                t = spread(turned[there, j : j + 1])
                a = a - t * spread(block[j : j + 1, :])
                b = b - t * spread(side[j : j + 1, :])
            work[there, left] = a
            work[there, right] = b
        if at + 2 * PANEL < size:
            there = slice(at + 2 * PANEL, size)
            update = dot(block, jnp.concatenate([block, side], axis=1), 0, 0, HIGHEST)
            work[there, :] = work[there, :] - update[there, :]
        hooks.pop(0)()


def inverse_factor(a, work, inv, hooks):
    n = a.shape[0]
    if n == BASE:
        i = lax.broadcasted_iota(jnp.int32, (n, n), 0)
        j = lax.broadcasted_iota(jnp.int32, (n, n), 1)
        work[...] = jnp.concatenate([a, (i == j).astype(F32)], axis=1)
        eliminate(work, inv, hooks)
        return inv[...]
    h = n // 2
    w11 = inverse_factor(a[:h, :h], work, inv, hooks)
    l21 = dot(a[h:, :h], w11, 1, 1, HIGHEST)
    w22 = inverse_factor(a[h:, h:] - dot(l21, l21, 1, 1, HIGHEST), work, inv, hooks)
    w21 = -dot(dot(w22, l21, 1, 0, HIGHEST), w11, 1, 0, HIGHEST)
    top = jnp.concatenate([w11, jnp.zeros((h, h), F32)], axis=1)
    return jnp.concatenate([top, jnp.concatenate([w21, w22], axis=1)], axis=0)


class Mail:
    def __init__(self, send, recv):
        self.send, self.recv, self.ids, self.started = send, recv, {}, {}

    def copy(self, key, src, dst, where):
        k = self.ids.setdefault(key, len(self.ids))
        return pltpu.make_async_remote_copy(
            src_ref=src, dst_ref=dst, send_sem=self.send.at[k], recv_sem=self.recv.at[k],
            device_id=where, device_id_type=MESH,
        )

    def start(self, key, src, dst, where, whole=None):
        self.copy(key, src() if callable(src) else src, dst, where).start()
        assert whole is not None or key not in self.started, key
        self.started[key] = (src if whole is None else whole, where)

    def take(self, key, dst, where):
        self.copy(key, dst, dst, where).wait_recv()

    def close(self):
        for key, (ref, where) in self.started.items():
            ref = ref() if callable(ref) else ref
            self.copy(key, ref, ref, where).wait_send()


def kernel(
    groups, count, border, inverse, prior_hbm, sel, asg, prob, panel, out,
    big, minv, prior, flat, rows, got1, got2, q0, qh, qx, qz, qv, qg, q, picked, project,
    corner, corner_got, corner_sum, ya, ya_s, ya_g, ya_sg, xb, xb_s, xb_g, xb_sg,
    xa, xa_s, xa_g, xa_sg, yb, yb_s, yb_g, yb_sg, keep0, solution_rows, keep_a, keep_b, hit, work, invb,
    pan, acc, sums, core_got, keep1, z_code, z_scale, z_got, z_sgot,
    load, send, recv,
):
    grp, dev = lax.axis_index("grp"), lax.axis_index("dev")
    depth = count // (CORES * XHI)
    z, xhi, core = dev // (CORES * XHI), (dev // CORES) % XHI, dev % CORES
    at = lambda zz, xx, cc: (grp, (zz * XHI + xx) * CORES + cc)
    cpart, xpart = at(z, xhi, 1 - core), at(z, 1 - xhi, core)
    zparts = {o: at((z + o) % depth, xhi, core) for o in range(1, depth)}
    far = sorted(range(depth), key=lambda o: -min(o, depth - o))
    chips = [(o, x) for o in far for x in (1, 0) if (o, x) != (0, 0)]
    chip = {c: at((z + c[0]) % depth, xhi ^ c[1], core) for c in chips}
    slot = {c: i for i, c in enumerate(chips)}
    ys = [y for y in (2, 1, 3) if y < groups // XLO]
    near = [o for o in (5, 4, 7, 6, 3, 2, 1) if o < groups]
    peer = {o: (grp ^ o, dev) for o in near}
    width, size = picked.shape
    own = prior.shape[0]
    mail = Mail(send, recv)

    def fenced(f, *args):
        pl.when(grp >= 0)(functools.partial(f, *args))

    loads = {o: pltpu.make_async_copy(border.at[pl.ds((grp ^ o) * own, own)], big.at[o], load.at[o]) for o in range(groups)}
    loads["prior"] = pltpu.make_async_copy(prior_hbm, prior, load.at[groups])
    loads["inverse"] = pltpu.make_async_copy(inverse, minv, load.at[groups + 1])
    for name in ["prior"] + list(range(groups)) + ["inverse"]:
        loads[name].start()
    barrier = pltpu.get_barrier_semaphore()
    partners = [cpart] + list(chip.values()) + list(peer.values())
    for where in partners:
        pl.semaphore_signal(barrier, inc=1, device_id=where, device_id_type=MESH)

    want = jnp.transpose(jnp.broadcast_to(sel[...], (LANES, width)))[:, :1]
    want = jnp.broadcast_to(want, (width, own))
    lanes = lax.broadcasted_iota(jnp.int32, (width, own), 1)
    first = (dev * groups + grp) * own
    loads["prior"].wait()
    mine = dot((want - first == lanes).astype(F32).astype(BF16), prior[...], 1, 0).astype(BF16)
    for c in range(2):
        q0[pl.ds(c * width, width), :] = mine[:, c * LANES : (c + 1) * LANES]
    total = None
    for o in range(groups):
        loads[o].wait()
        base = (dev * groups + (grp ^ o)) * own
        part = dot((want - base == lanes).astype(F32).astype(BF16), big[o], 1, 0)
        total = part if total is None else total + part
    total = total.astype(BF16)
    for c in range(size // LANES):
        flat[pl.ds(c * width, width), :] = total[:, c * LANES : (c + 1) * LANES]
    pl.semaphore_wait(barrier, len(partners))

    high = flat.shape[0]
    half, quarter, bit = high // CORES, high // (CORES * XHI), high // count
    qhalf, qquart, qbit = 2 * width // CORES, 2 * width // (CORES * XHI), 2 * width // count
    at1 = core * half
    at3 = at1 + xhi * quarter + z * bit
    qat1 = core * qhalf
    qat2 = qat1 + xhi * qquart
    qat3 = qat2 + z * qbit
    mail.start("r1", flat.at[pl.ds((1 - core) * half, half)], got1, cpart)
    mail.start("q1", q0.at[pl.ds((1 - core) * qhalf, qhalf)], qh, cpart)
    mail.take("r1", got1, cpart)
    flat[pl.ds(at1, half), :] = flat[pl.ds(at1, half), :] + got1[...]
    for c in chips:
        there = at1 + (xhi ^ c[1]) * quarter + ((z + c[0]) % depth) * bit
        mail.start("r2", flat.at[pl.ds(there, bit)], got2.at[slot[c]], chip[c], got2)
    mail.take("q1", qh, cpart)
    q0[pl.ds(qat1, qhalf), :] = q0[pl.ds(qat1, qhalf), :] + qh[...]
    mail.start("q2", q0.at[pl.ds(qat1 + (1 - xhi) * qquart, qquart)], qx, xpart)
    ids = first + lax.broadcasted_iota(jnp.int32, (own, width), 0)
    marked = jnp.max((ids == sel[...]).astype(F32), axis=1, keepdims=True)
    hit[...] = jnp.broadcast_to(marked, hit.shape)
    mail.take("q2", qx, xpart)
    q0[pl.ds(qat2, qquart), :] = q0[pl.ds(qat2, qquart), :] + qx[...]
    for o in zparts:
        mail.start("q3", q0.at[pl.ds(qat2 + ((z + o) % depth) * qbit, qbit)], qz.at[o - 1], zparts[o], qz)
    mail.take("r2", got2, xpart)
    value = flat[pl.ds(at3, bit), :]
    for c in chips:
        value = value + got2[slot[c]]
    rows[pl.ds(at3, bit), :] = value
    here = rows.at[pl.ds(at3, bit)]
    rings = [chips[i : i + 5] for i in range(0, len(chips), 5)]
    for n, ring in enumerate(rings):
        for c in ring:
            mail.start(("r3", n), here, here, chip[c], got2.at[pl.ds(0, len(ring))])
    other = rows.at[pl.ds((1 - core) * half, half)]
    mail.start("r4", here, here, cpart, other)
    value = q0[pl.ds(qat3, qbit), :]
    if zparts:
        mail.take("q3", qz, xpart)
    for o in zparts:
        value = value + qz[o - 1]
    qv[...] = value
    for n, o in enumerate(near):
        mail.start("q4", qv, qg.at[n], peer[o], qg)

    def forward(n):
        mail.take(("r3", n), got2.at[pl.ds(0, len(rings[n]))], xpart)
        for c in rings[n]:
            there = rows.at[pl.ds(at1 + (xhi ^ c[1]) * quarter + ((z + depth - c[0]) % depth) * bit, bit)]
            mail.start("r4", there, there, cpart, other)

    order = list(range(len(rings)))[::-1]
    forward(order[0])
    mail.take("q4", qg, xpart)
    value = qv[...]
    for n in range(len(near)):
        value = value + qg[n]
    q[pl.ds(qat3, qbit), :] = value
    here = q.at[pl.ds(qat3, qbit)]
    mail.start("q5", here, here, xpart)
    for n in order[1:]:
        forward(n)
    mail.take("r4", other, cpart)

    for c in range(size // LANES):
        picked[:, c * LANES : (c + 1) * LANES] = rows[pl.ds(c * width, width), :]
    loads["inverse"].wait()
    project[...] = dot(minv[...], picked[...], 1, 1).astype(BF16)
    scenario = asg[grp]
    weight = 0.0
    for i in range(groups):
        weight = weight + jnp.where(scenario == i, prob[i], 0.0)
    turn = min(4, depth)
    steps = {4: (2, 1, depth - 1), 2: (1,), 1: ()}[turn]
    chalf, cpiece = width // CORES, width // CORES // turn
    cmine = pl.ds(core * chalf + z % turn * cpiece, cpiece)
    corner[...] = weight * dot(picked[cmine, :], project[...], 1, 0)
    for n, o in enumerate(near):
        mail.start("c1", corner, corner_got.at[n], peer[o], corner_got)
    ra, rb = split(own, 0.56)

    def block(o):
        return weight * jnp.dot(big[o], project[...], preferred_element_type=F32)

    def make(y):
        side = block(2 * y + 1)
        encode(side[ra:], xb.at[y], xb_s.at[y])
        if y:
            encode(side[:ra], ya.at[y, 1], ya_s.at[y, 1])
            same = block(2 * y)
            encode(same[:ra], ya.at[y, 0], ya_s.at[y, 0])
            keep_b[y] = same[ra:]
        else:
            keep_a[...] = side[:ra]

    def ship(y):
        mail.start(("xbs", y), lambda: xb_s.at[y], xb_sg.at[y], peer[1])
        mail.start(("xb", y), lambda: xb.at[y], xb_g.at[y], peer[1])
        if y:
            mail.start(("yas", y), lambda: ya_s.at[y], ya_sg.at[y], peer[2 * y])
            mail.start(("ya", y), lambda: ya.at[y], ya_g.at[y], peer[2 * y])

    lots = q.at[pl.ds(0, XHI * (depth - 1) * qbit)]
    rest = corner_sum.at[pl.ds(0, (turn - 1) * cpiece)]

    def blocks(y):
        make(y)
        ship(y)

    def corner_out():
        mail.take("c1", corner_got, xpart)
        value = corner[...]
        for n in range(len(near)):
            value = value + corner_got[n]
        corner_sum[cmine, :] = value
        here = corner_sum.at[cmine]
        for o in steps:
            mail.start("c2", here, here, zparts[o], lambda: rest)

    def prior_out():
        mail.take("q5", q.at[pl.ds(qat1 + (1 - xhi) * qquart + z * qbit, qbit)], xpart)
        for o in zparts:
            for x in range(XHI):
                here = q.at[pl.ds(qat1 + x * qquart + z * qbit, qbit)]
                mail.start("q6", here, here, zparts[o], lambda: lots)

    def prior_over():
        if zparts:
            mail.take("q6", lots, xpart)
        here = lambda: q.at[pl.ds(qat1, qhalf)]
        mail.start("q7", here, here(), cpart)

    for y in ys[:1]:
        fenced(blocks, y)
    fenced(prior_out)
    for y in ys[1:2]:
        fenced(blocks, y)
    fenced(corner_out)
    for y in ys[2:] + [0]:
        fenced(blocks, y)
    fenced(prior_over)
    keep0[...] = block(0)
    mail.take("q7", q.at[pl.ds((1 - core) * qhalf, qhalf)], cpart)
    picks = jnp.concatenate([q[pl.ds(c * width, width), :] for c in range(2)], axis=1)
    keep0[...] -= dot(prior[...], picks, 1, 1)
    less = dot(picks, picks, 1, 1)
    if zparts:
        mail.take("c2", rest, xpart)
    here = corner_sum.at[pl.ds(core * chalf, chalf)]
    mail.start("c3", here, here, cpart)
    mail.take("c3", corner_sum.at[pl.ds((1 - core) * chalf, chalf)], cpart)
    a = corner_sum[...] - less
    a = 0.5 * (a + jnp.transpose(a))

    def onward(y):
        mail.take(("xbs", y), xb_sg.at[y], peer[1])
        mail.take(("xb", y), xb_g.at[y], peer[1])
        encode(keep_b[y] + decode(xb_g[y], xb_sg[y]), yb.at[y], yb_s.at[y])
        mail.start(("ybs", y), lambda: yb_s.at[y], yb_sg.at[y], peer[2 * y])
        mail.start(("yb", y), lambda: yb.at[y], yb_g.at[y], peer[2 * y])

    def across():
        value, here = keep_a[...], keep0[:ra, :]
        for y in ys:
            mail.take(("yas", y), ya_sg.at[y], peer[2 * y])
            mail.take(("ya", y), ya_g.at[y], peer[2 * y])
            value = value + decode(ya_g[y, 1], ya_sg[y, 1])
            here = here + decode(ya_g[y, 0], ya_sg[y, 0])
        encode(value, xa, xa_s)
        mail.start("xas", xa_s, xa_sg, peer[1])
        mail.start("xa", xa, xa_g, peer[1])
        keep0[:ra, :] = here

    def gather():
        mail.take("xas", xa_sg, peer[1])
        mail.take("xa", xa_g, peer[1])
        mail.take(("xbs", 0), xb_sg.at[0], peer[1])
        mail.take(("xb", 0), xb_g.at[0], peer[1])
        keep0[:ra, :] = keep0[:ra, :] + decode(xa_g[...], xa_sg[...])
        lower = keep0[ra:, :] + decode(xb_g[0], xb_sg[0])
        for y in ys:
            mail.take(("ybs", y), yb_sg.at[y], peer[2 * y])
            mail.take(("yb", y), yb_g.at[y], peer[2 * y])
            lower = lower + decode(yb_g[y], yb_sg[y])
        keep0[ra:, :] = lower

    hooks = [lambda: None for _ in range(width // PANEL)]
    for y, n in zip(ys, (0, 1, 4)):
        hooks[n] = functools.partial(fenced, onward, y)
    hooks[7] = functools.partial(fenced, across)
    hooks[15] = functools.partial(fenced, gather)
    w = inverse_factor(a, work, invb, hooks)

    pa, pb = split(own, 0.53)
    top, low = pl.ds(0, pa), pl.ds(pa, pb)

    def solve(rows):
        solved = dot(keep0[rows, :], w, 1, 1, HIGHEST)
        solved = jnp.where(hit[rows, :] > 0.5, 0.0, solved)
        solution_rows[rows, :] = solved
        pan[0, rows, :] = solved.astype(BF16)

    tops = [pl.ds(0, pa // 32 * 16), pl.ds(pa // 32 * 16, pa - pa // 32 * 16)]
    lows = [pl.ds(pa, pb // 32 * 16), pl.ds(pa + pb // 32 * 16, pb - pb // 32 * 16)]
    ends = [y for y in (1, 3) if y < groups // XLO]
    relay = 2 in ys

    def add(o):
        acc[...] += dot(pan[o], big[o], 0, 0)

    def pass_on(kind, y, x, pieces, n):
        if relay:
            mail.start((kind, n), pan.at[2 * y + x, pieces[n]], pan.at[4 + x, pieces[n]], peer[2 * (y ^ 2)])

    def passed(kind, x, pieces):
        for n in range(2):
            mail.take((kind, n), pan.at[4 + x, pieces[n]], peer[2 * ends[1 - n]])

    solve(slice(0, pa))
    for y in ends:
        mail.start(("g2", y), pan.at[0, top], pan.at[2 * y, top], peer[2 * y])
    solve(slice(pa, own))
    mail.start("g1", pan.at[0, low], pan.at[1, low], peer[1])
    mail.start("g3", pan.at[0, top], pan.at[1, top], peer[1])
    for y in ends:
        mail.start(("g4", y), pan.at[0, low], pan.at[2 * y, low], peer[2 * y])
    written = pltpu.make_async_copy(solution_rows, panel, load.at[groups])
    written.start()
    acc[...] = dot(pan[0], big[0], 0, 0)
    for n, y in enumerate(ends):
        mail.take(("g2", y), pan.at[2 * y, top], peer[2 * y])
        pass_on("h2", y, 0, tops, n)
        mail.start(("g6", y), pan.at[2 * y, top], pan.at[2 * y + 1, top], peer[1])
    mail.take("g1", pan.at[1, low], peer[1])
    for y in ends:
        mail.start(("g5", y), pan.at[1, low], pan.at[2 * y + 1, low], peer[2 * y])
    for n, y in enumerate(ends):
        mail.take(("g4", y), pan.at[2 * y, low], peer[2 * y])
        pass_on("h4", y, 0, lows, n)
    mail.take("g3", pan.at[1, top], peer[1])
    add(1)
    if relay:
        passed("h2", 0, tops)
        mail.start(("g6", 2), pan.at[4, top], pan.at[5, top], peer[1])
    for y in ends:
        add(2 * y)
    for n, y in enumerate(ends):
        mail.take(("g5", y), pan.at[2 * y + 1, low], peer[2 * y])
        pass_on("h5", y, 1, lows, n)
    for y in ends:
        mail.take(("g6", y), pan.at[2 * y + 1, top], peer[1])
        add(2 * y + 1)
    if relay:
        passed("h4", 0, lows)
        add(4)
        mail.take(("g6", 2), pan.at[5, top], peer[1])
        passed("h5", 1, lows)
        add(5)

    piece = sums.shape[3]
    scale = 1.0 / math.sqrt(N1)
    halves = [range(0, (depth + 1) // 2), range((depth + 1) // 2, depth)]
    halves = [h for h in halves if len(h)]
    tiles = acc.shape[1] // LANES
    done = 0
    for e in range(tiles):
        turned = jnp.transpose(acc[:, e * LANES : (e + 1) * LANES]) * scale
        for k in range(LANES // piece):
            n = e * (LANES // piece) + k
            zz, xx, cc = n // (XHI * CORES), (n // CORES) % XHI, n % CORES
            sums[cc, zz, xx] = turned[k * piece : (k + 1) * piece, :]
        if done < len(halves) and n + 1 == len(halves[done]) * XHI * CORES + (halves[done][0]) * XHI * CORES:
            part = pl.ds(halves[done][0], len(halves[done]))
            mail.start(("s1", done), sums.at[1 - core, part], core_got.at[part], cpart)
            done += 1
    assert done == len(halves)
    for n, h in enumerate(halves):
        mail.take(("s1", n), core_got.at[pl.ds(h[0], len(h))], cpart)
    value = (sums[core] + core_got[...]).reshape(depth * XHI * piece, width)
    keep1[...] = value.reshape(keep1.shape)
    peak = jnp.maximum(jnp.max(jnp.abs(value), axis=0, keepdims=True), 1e-30)
    z_scale[...] = peak * (1.0 / TOP)
    z_code[...] = jnp.round(value * (TOP / peak)).astype(jnp.int32).astype(I16).reshape(z_code.shape)
    for c in chips:
        mail.start("s2s", z_scale, z_sgot.at[slot[c]], chip[c], z_sgot)
        mail.start("s2", z_code.at[(z + c[0]) % depth, xhi ^ c[1]], z_got.at[slot[c]], chip[c], z_got)
    mail.take("s2s", z_sgot, xpart)
    mail.take("s2", z_got, xpart)
    value = keep1[z, xhi]
    for n in range(len(chips)):
        value = value + decode(z_got[n], z_sgot[n])
    out[...] = value
    written.wait()
    mail.close()
    assert len(mail.ids) <= send.shape[0], len(mail.ids)


def call(groups, count, border, inverse, prior, sel, asg, prob):
    size = border.shape[1]
    own, width = prior.shape
    depth = count // (CORES * XHI)
    messages = 59
    n = max(depth - 1, 1)
    others = depth * XHI - 1
    piece = size // count
    high = size // LANES * width
    ny = groups // XLO
    ra, rb = split(own, 0.56)
    dma, vmem = pltpu.SemaphoreType.DMA, pltpu.VMEM
    vm = pl.BlockSpec(memory_space=vmem)
    anyspace = pl.BlockSpec(memory_space=pl.ANY)
    sm = pl.BlockSpec(memory_space=pltpu.SMEM)
    return pl.pallas_call(
        functools.partial(kernel, groups, count),
        out_shape=(jax.ShapeDtypeStruct((own, width), F32), jax.ShapeDtypeStruct((piece, width), F32)),
        in_specs=[anyspace, anyspace, anyspace, vm, sm, sm],
        out_specs=(anyspace, vm),
        scratch_shapes=[
            vmem((groups, own, size), BF16),
            vmem((size, size), BF16),
            vmem((own, width), BF16),
            vmem((high, LANES), BF16),
            vmem((high, LANES), BF16),
            vmem((high // CORES, LANES), BF16),
            vmem((others, high // count, LANES), BF16),
            vmem((2 * width, LANES), BF16),
            vmem((2 * width // CORES, LANES), BF16),
            vmem((2 * width // (CORES * XHI), LANES), BF16),
            vmem((n, 2 * width // count, LANES), BF16),
            vmem((2 * width // count, LANES), BF16),
            vmem((groups - 1, 2 * width // count, LANES), BF16),
            vmem((2 * width, LANES), BF16),
            vmem((width, size), BF16),
            vmem((size, width), BF16),
            vmem((width // CORES // min(4, depth), width), F32),
            vmem((groups - 1, width // CORES // min(4, depth), width), F32),
            vmem((width, width), F32),
            vmem((ny, 2, ra, width), I16),
            vmem((ny, 2, 1, width), F32),
            vmem((ny, 2, ra, width), I16),
            vmem((ny, 2, 1, width), F32),
            vmem((ny, rb, width), I16),
            vmem((ny, 1, width), F32),
            vmem((ny, rb, width), I16),
            vmem((ny, 1, width), F32),
            vmem((ra, width), I16),
            vmem((1, width), F32),
            vmem((ra, width), I16),
            vmem((1, width), F32),
            vmem((ny, rb, width), I16),
            vmem((ny, 1, width), F32),
            vmem((ny, rb, width), I16),
            vmem((ny, 1, width), F32),
            vmem((own, width), F32),
            vmem((own, width), F32),
            vmem((ra, width), F32),
            vmem((ny, rb, width), F32),
            vmem((own, width), F32),
            vmem((BASE, 2 * BASE), F32),
            vmem((BASE, BASE), F32),
            vmem((groups, own, width), BF16),
            vmem((width, size), F32),
            vmem((CORES, depth, XHI, piece, width), F32),
            vmem((depth, XHI, piece, width), F32),
            vmem((depth, XHI, piece, width), F32),
            vmem((depth, XHI, piece, width), I16),
            vmem((1, width), F32),
            vmem((others, piece, width), I16),
            vmem((others, 1, width), F32),
            dma((groups + 2,)),
            dma((messages,)),
            dma((messages,)),
        ],
        compiler_params=pltpu.CompilerParams(
            collective_id=0, has_side_effects=True, vmem_limit_bytes=60 << 20
        ),
        name="panel",
    )(border, inverse, prior, sel, asg, prob)


def finish_kernel(panel, residual, panel_out, residual_out):
    panel_out[...] = panel[...]
    residual_out[...] = residual[...]


def finish(panel, residual):
    vm = pl.BlockSpec(memory_space=pltpu.VMEM)
    return pl.pallas_call(
        finish_kernel,
        out_shape=(jax.ShapeDtypeStruct(panel.shape, F32), jax.ShapeDtypeStruct(residual.shape, F32)),
        in_specs=[vm, vm],
        out_specs=(vm, vm),
        name="finish",
    )(panel, residual)


def body(border, inverse_blocks, selected, assignment, probability, prior_panel):
    groups, count = lax.axis_size("grp"), lax.axis_size("dev")
    panel, residual = call(
        groups, count, border[0], inverse_blocks[0], prior_panel, selected[None, :], assignment, probability
    )
    panel, residual = finish(panel, residual)
    return (panel, residual[None])


def solution(mesh):
    return jax.shard_map(
        body,
        mesh=mesh,
        in_specs=(
            P("grp", "dev", None),
            P("grp", None, None),
            P(),
            P(),
            P(),
            P(("dev", "grp"), None),
        ),
        out_specs=(P(("dev", "grp"), None), P("grp", "dev", None)),
        check_vma=False,
    )
```

```python
import functools
import math

import jax
import jax.numpy as jnp
from jax import lax
from jax.experimental import pallas as pl
from jax.experimental.pallas import tpu as pltpu
from jax.sharding import PartitionSpec as P

N1 = 131072
MESH = pl.DeviceIdType.MESH
HIGHEST = lax.Precision.HIGHEST
F32 = jnp.float32
BF16 = jnp.bfloat16
I16 = jnp.int16
LANES = 128
CORES, XHI, XLO = 2, 2, 2
TOP = 32767.0
BASE, PANEL = 128, 16


def dot(a, b, ca, cb, precision=None):
    return lax.dot_general(
        a, b, (((ca,), (cb,)), ((), ())), precision=precision, preferred_element_type=F32
    )


def split(own, share):
    part = max(16, int(own * share / 16 + 0.5) * 16)
    return own - part, part


def encode(x, code, scale):
    peak = jnp.maximum(jnp.max(jnp.abs(x), axis=0, keepdims=True), 1e-30)
    code[...] = jnp.round(x * (TOP / peak)).astype(jnp.int32).astype(I16)
    scale[...] = peak * (1.0 / TOP)


def decode(code, scale):
    return code.astype(jnp.int32).astype(F32) * scale


def eliminate(work, inv, hooks):
    size = work.shape[0]
    shape = (PANEL, size)
    row = lax.broadcasted_iota(jnp.int32, shape, 0)
    spread = lambda x: jnp.broadcast_to(x, shape)
    left, right = slice(0, size), slice(size, 2 * size)
    for at in range(0, size, PANEL):
        here = slice(at, at + PANEL)
        block, side = work[here, left], work[here, right]
        cs = [spread(block[:, at + j : at + j + 1]) for j in range(PANEL)]
        pivots = jnp.zeros(shape, F32)
        for j in range(PANEL):
            pivots = jnp.where(row == j, cs[j], pivots)
            m = jnp.where(row > j, cs[j] * spread(1.0 / cs[j][j : j + 1, :]), 0.0)
            for k in range(j + 1, PANEL):
                cs[k] = cs[k] - m * spread(cs[k][j : j + 1, :])
            block = block - m * spread(block[j : j + 1, :])
            side = side - m * spread(side[j : j + 1, :])
        r = lax.rsqrt(pivots)
        r = r * (1.5 - 0.5 * pivots * r * r)
        block, side = block * r, side * r
        inv[here, :] = side
        turned = jnp.transpose(block)
        if at + PANEL < size:
            there = slice(at + PANEL, at + 2 * PANEL)
            a, b = work[there, left], work[there, right]
            for j in range(PANEL):
                t = spread(turned[there, j : j + 1])
                a = a - t * spread(block[j : j + 1, :])
                b = b - t * spread(side[j : j + 1, :])
            work[there, left] = a
            work[there, right] = b
        if at + 2 * PANEL < size:
            there = slice(at + 2 * PANEL, size)
            update = dot(block, jnp.concatenate([block, side], axis=1), 0, 0, HIGHEST)
            work[there, :] = work[there, :] - update[there, :]
        hooks.pop(0)()


def eliminated(a, work, inv, hooks):
    n = a.shape[0]
    i = lax.broadcasted_iota(jnp.int32, (n, n), 0)
    j = lax.broadcasted_iota(jnp.int32, (n, n), 1)
    work[...] = jnp.concatenate([a, (i == j).astype(F32)], axis=1)
    eliminate(work, inv, hooks)
    return inv[...]


class Mail:
    def __init__(self, send, recv):
        self.send, self.recv, self.ids, self.started = send, recv, {}, {}

    def copy(self, key, src, dst, where):
        k = self.ids.setdefault(key, len(self.ids))
        return pltpu.make_async_remote_copy(
            src_ref=src, dst_ref=dst, send_sem=self.send.at[k], recv_sem=self.recv.at[k],
            device_id=where, device_id_type=MESH,
        )

    def start(self, key, src, dst, where, whole=None):
        self.copy(key, src() if callable(src) else src, dst, where).start()
        assert whole is not None or key not in self.started, key
        self.started[key] = (src if whole is None else whole, where)

    def take(self, key, dst, where):
        self.copy(key, dst, dst, where).wait_recv()

    def close(self):
        for key, (ref, where) in self.started.items():
            ref = ref() if callable(ref) else ref
            self.copy(key, ref, ref, where).wait_send()


def kernel(
    groups, count, border, inverse, prior_hbm, sel_hbm, asg_hbm, prob_hbm, panel, out,
    sel, asg, prob, last, big, minv, prior, flat, rows, hot, got1, got2, q0, qh, qx, qz, qv, qg, q, picked, project,
    corner, corner_got, corner_sum, ya, ya_s, ya_g, ya_sg, xb, xb_s, xb_g, xb_sg,
    xa, xa_s, xa_g, xa_sg, yb, yb_s, yb_g, yb_sg, keep0, solution_rows, keep_a, keep_b, hit, work, invb, inv1, cross,
    pan, acc, sums, core_got, keep1, z_code, z_scale, z_got, z_sgot,
    load, send, recv,
):
    grp, dev = lax.axis_index("grp"), lax.axis_index("dev")
    depth = count // (CORES * XHI)
    z, xhi, core = dev // (CORES * XHI), (dev // CORES) % XHI, dev % CORES
    at = lambda zz, xx, cc: (grp, (zz * XHI + xx) * CORES + cc)
    cpart, xpart = at(z, xhi, 1 - core), at(z, 1 - xhi, core)
    zparts = {o: at((z + o) % depth, xhi, core) for o in range(1, depth)}
    far = sorted(range(depth), key=lambda o: -min(o, depth - o))
    chips = [(o, x) for o in far for x in (1, 0) if (o, x) != (0, 0)]
    chip = {c: at((z + c[0]) % depth, xhi ^ c[1], core) for c in chips}
    slot = {c: i for i, c in enumerate(chips)}
    ys = [y for y in (2, 1, 3) if y < groups // XLO]
    near = [o for o in (5, 4, 7, 6, 3, 2, 1) if o < groups]
    peer = {o: (grp ^ o, dev) for o in near}
    width, size = picked.shape
    own = prior.shape[0]
    mail = Mail(send, recv)

    def fenced(f, *args):
        pl.when(grp >= 0)(functools.partial(f, *args))

    loads = {o: pltpu.make_async_copy(border.at[pl.ds((grp ^ o) * own, own)], big.at[o], load.at[o]) for o in range(groups)}
    loads["prior"] = pltpu.make_async_copy(prior_hbm, prior, load.at[groups])
    loads["inverse"] = pltpu.make_async_copy(inverse, minv, load.at[groups + 1])
    loads["sel"] = pltpu.make_async_copy(sel_hbm, sel, load.at[groups + 2])
    loads["asg"] = pltpu.make_async_copy(asg_hbm, asg, load.at[groups + 3])
    loads["prob"] = pltpu.make_async_copy(prob_hbm, prob, load.at[groups + 4])
    for name in ["sel"] + list(range(groups)) + ["prior", "inverse", "asg", "prob"]:
        loads[name].start()
    barrier = pltpu.get_barrier_semaphore()
    partners = [cpart] + list(chip.values()) + list(peer.values())
    for where in partners:
        pl.semaphore_signal(barrier, inc=1, device_id=where, device_id_type=MESH)

    loads["sel"].wait()
    want = jnp.transpose(jnp.broadcast_to(sel[...], (LANES, width)))[:, :1]
    want = jnp.broadcast_to(want, (width, own))
    lanes = lax.broadcasted_iota(jnp.int32, (width, own), 1)
    first = (dev * groups + grp) * own
    high = flat.shape[0]
    half, quarter, bit = high // CORES, high // (CORES * XHI), high // count
    at1 = core * half
    part = size // CORES

    def pick(which):
        total = None
        at = pl.multiple_of(which * part, LANES)
        for o in range(groups):
            if which is not core:
                loads[o].wait()
                base = (dev * groups + (grp ^ o)) * own
                hot[o] = (want - base == lanes).astype(F32).astype(BF16)
            got = dot(hot[o], big[o, :, pl.ds(at, part)], 1, 0)
            total = got if total is None else total + got
        total = total.astype(BF16)
        for c in range(part // LANES):
            flat[pl.ds(which * half + c * width, width), :] = total[:, c * LANES : (c + 1) * LANES]

    pick(1 - core)
    pl.semaphore_wait(barrier, len(partners))
    fenced(lambda: mail.start("r1", lambda: flat.at[pl.ds((1 - core) * half, half)], got1, cpart))
    pick(core)
    loads["prior"].wait()
    mine = dot((want - first == lanes).astype(F32).astype(BF16), prior[...], 1, 0).astype(BF16)
    for c in range(2):
        q0[pl.ds(c * width, width), :] = mine[:, c * LANES : (c + 1) * LANES]

    qhalf, qquart, qbit = 2 * width // CORES, 2 * width // (CORES * XHI), 2 * width // count
    at3 = at1 + xhi * quarter + z * bit
    qat1 = core * qhalf
    qat2 = qat1 + xhi * qquart
    qat3 = qat2 + z * qbit
    mail.start("q1", q0.at[pl.ds((1 - core) * qhalf, qhalf)], qh, cpart)
    mail.take("r1", got1, cpart)
    flat[pl.ds(at1, half), :] = flat[pl.ds(at1, half), :] + got1[...]
    for c in chips:
        there = at1 + (xhi ^ c[1]) * quarter + ((z + c[0]) % depth) * bit
        mail.start("r2", flat.at[pl.ds(there, bit)], got2.at[slot[c]], chip[c], got2)
    mail.take("q1", qh, cpart)
    q0[pl.ds(qat1, qhalf), :] = q0[pl.ds(qat1, qhalf), :] + qh[...]
    mail.start("q2", q0.at[pl.ds(qat1 + (1 - xhi) * qquart, qquart)], qx, xpart)
    ids = first + lax.broadcasted_iota(jnp.int32, (own, width), 0)
    marked = jnp.max((ids == sel[...]).astype(F32), axis=1, keepdims=True)
    hit[...] = jnp.broadcast_to(marked, hit.shape)
    mail.take("q2", qx, xpart)
    q0[pl.ds(qat2, qquart), :] = q0[pl.ds(qat2, qquart), :] + qx[...]
    for o in zparts:
        mail.start("q3", q0.at[pl.ds(qat2 + ((z + o) % depth) * qbit, qbit)], qz.at[o - 1], zparts[o], qz)
    mail.take("r2", got2, xpart)
    value = flat[pl.ds(at3, bit), :]
    for c in chips:
        value = value + got2[slot[c]]
    rows[pl.ds(at3, bit), :] = value
    here = rows.at[pl.ds(at3, bit)]
    rings = [chips[i : i + 5] for i in range(0, len(chips), 5)]
    for n, ring in enumerate(rings):
        for c in ring:
            mail.start(("r3", n), here, here, chip[c], got2.at[pl.ds(0, len(ring))])
    other = rows.at[pl.ds((1 - core) * half, half)]
    mail.start("r4", here, here, cpart, other)
    value = q0[pl.ds(qat3, qbit), :]
    if zparts:
        mail.take("q3", qz, xpart)
    for o in zparts:
        value = value + qz[o - 1]
    qv[...] = value
    for n, o in enumerate(near):
        mail.start("q4", qv, qg.at[n], peer[o], qg)

    def forward(n):
        mail.take(("r3", n), got2.at[pl.ds(0, len(rings[n]))], xpart)
        for c in rings[n]:
            there = rows.at[pl.ds(at1 + (xhi ^ c[1]) * quarter + ((z + depth - c[0]) % depth) * bit, bit)]
            mail.start("r4", there, there, cpart, other)

    order = list(range(len(rings)))[::-1]
    forward(order[0])
    mail.take("q4", qg, xpart)
    value = qv[...]
    for n in range(len(near)):
        value = value + qg[n]
    q[pl.ds(qat3, qbit), :] = value
    here = q.at[pl.ds(qat3, qbit)]
    mail.start("q5", here, here, xpart)
    for n in order[1:]:
        forward(n)
    mail.take("r4", other, cpart)

    for c in range(size // LANES):
        picked[:, c * LANES : (c + 1) * LANES] = rows[pl.ds(c * width, width), :]
    loads["inverse"].wait()
    project[...] = dot(minv[...], picked[...], 1, 1).astype(BF16)
    loads["asg"].wait()
    loads["prob"].wait()
    scenario = asg[grp]
    weight = 0.0
    for i in range(groups):
        weight = weight + jnp.where(scenario == i, prob[i], 0.0)
    turn = min(4, depth)
    steps = {4: (2, 1, depth - 1), 2: (1,), 1: ()}[turn]
    chalf, cpiece = width // CORES, width // CORES // turn
    cmine = pl.ds(core * chalf + z % turn * cpiece, cpiece)
    corner[...] = weight * dot(picked[cmine, :], project[...], 1, 0)
    for n, o in enumerate(near):
        mail.start("c1", corner, corner_got.at[n], peer[o], corner_got)
    ra, rb = split(own, 0.53)

    def block(o):
        return weight * jnp.dot(big[o], project[...], preferred_element_type=F32)

    def make(y):
        side = block(2 * y + 1)
        encode(side[ra:], xb.at[y], xb_s.at[y])
        if y:
            encode(side[:ra], ya.at[y, 1], ya_s.at[y, 1])
            same = block(2 * y)
            encode(same[:ra], ya.at[y, 0], ya_s.at[y, 0])
            keep_b[y] = same[ra:]
        else:
            keep_a[...] = side[:ra]

    def ship(y):
        mail.start(("xbs", y), lambda: xb_s.at[y], xb_sg.at[y], peer[1])
        mail.start(("xb", y), lambda: xb.at[y], xb_g.at[y], peer[1])
        if y:
            mail.start(("yas", y), lambda: ya_s.at[y], ya_sg.at[y], peer[2 * y])
            mail.start(("ya", y), lambda: ya.at[y], ya_g.at[y], peer[2 * y])

    lots = q.at[pl.ds(0, XHI * (depth - 1) * qbit)]
    rest = corner_sum.at[pl.ds(0, (turn - 1) * cpiece)]

    chalves = lambda: corner_sum.at[pl.ds(0, chalf)]

    def blocks(y):
        make(y)
        ship(y)

    def corner_out():
        mail.take("c1", corner_got, xpart)
        value = corner[...]
        for n in range(len(near)):
            value = value + corner_got[n]
        corner_sum[cmine, :] = value
        here = corner_sum.at[cmine]
        for o in steps:
            mail.start("c2", here, here, zparts[o], lambda: rest)
        mail.start("c3", here, here, cpart, chalves)

    def prior_out():
        mail.take("q5", q.at[pl.ds(qat1 + (1 - xhi) * qquart + z * qbit, qbit)], xpart)
        for o in zparts:
            for x in range(XHI):
                here = q.at[pl.ds(qat1 + x * qquart + z * qbit, qbit)]
                mail.start("q6", here, here, zparts[o], lambda: lots)

    def prior_over():
        if zparts:
            mail.take("q6", lots, xpart)
        here = lambda: q.at[pl.ds(qat1, qhalf)]
        mail.start("q7", here, here(), cpart)

    for y in ys[:1]:
        fenced(blocks, y)
    fenced(prior_out)
    for y in ys[1:2]:
        fenced(blocks, y)
    fenced(corner_out)
    for y in ys[2:] + [0]:
        fenced(blocks, y)
    fenced(prior_over)
    keep0[...] = block(0)
    mail.take("q7", q.at[pl.ds((1 - core) * qhalf, qhalf)], cpart)
    picks = jnp.concatenate([q[pl.ds(c * width, width), :] for c in range(2)], axis=1)
    keep0[...] -= dot(prior[...], picks, 1, 1)
    less = dot(picks, picks, 1, 1)
    if zparts:
        mail.take("c2", rest, xpart)
    for o in range(1, turn):
        here = corner_sum.at[pl.ds(core * chalf + (z + o) % turn * cpiece, cpiece)]
        mail.start("c3", here, here, cpart, chalves)
    mail.take("c3", corner_sum.at[pl.ds((1 - core) * chalf, chalf)], cpart)
    a = corner_sum[...] - less
    a = 0.5 * (a + jnp.transpose(a))

    def onward(y):
        mail.take(("xbs", y), xb_sg.at[y], peer[1])
        mail.take(("xb", y), xb_g.at[y], peer[1])
        encode(keep_b[y] + decode(xb_g[y], xb_sg[y]), yb.at[y], yb_s.at[y])
        mail.start(("ybs", y), lambda: yb_s.at[y], yb_sg.at[y], peer[2 * y])
        mail.start(("yb", y), lambda: yb.at[y], yb_g.at[y], peer[2 * y])

    def across():
        value, here = keep_a[...], keep0[:ra, :]
        for y in ys:
            mail.take(("yas", y), ya_sg.at[y], peer[2 * y])
            mail.take(("ya", y), ya_g.at[y], peer[2 * y])
            value = value + decode(ya_g[y, 1], ya_sg[y, 1])
            here = here + decode(ya_g[y, 0], ya_sg[y, 0])
        encode(value, xa, xa_s)
        mail.start("xas", xa_s, xa_sg, peer[1])
        mail.start("xa", xa, xa_g, peer[1])
        keep0[:ra, :] = here

    def gather():
        mail.take("xas", xa_sg, peer[1])
        mail.take("xa", xa_g, peer[1])
        mail.take(("xbs", 0), xb_sg.at[0], peer[1])
        mail.take(("xb", 0), xb_g.at[0], peer[1])
        keep0[:ra, :] = keep0[:ra, :] + decode(xa_g[...], xa_sg[...])
        lower = keep0[ra:, :] + decode(xb_g[0], xb_sg[0])
        for y in ys:
            mail.take(("ybs", y), yb_sg.at[y], peer[2 * y])
            mail.take(("yb", y), yb_g.at[y], peer[2 * y])
            lower = lower + decode(yb_g[y], yb_sg[y])
        keep0[ra:, :] = lower
        whole = jnp.where(hit[...] > 0.5, 0.0, keep0[...])
        left = dot(whole[:, :BASE], inv1[...], 1, 1, HIGHEST)
        solution_rows[:, :BASE] = left
        pan[0, :, :BASE] = left.astype(BF16)
        keep0[:, BASE:] = whole[:, BASE:] - dot(left, cross[...], 1, 1, HIGHEST)

    hooks = [lambda: None for _ in range(width // PANEL)]
    for y, n in zip(ys, (0, 1, 4)):
        hooks[n] = functools.partial(fenced, onward, y)
    hooks[7] = functools.partial(fenced, across)
    hooks[15] = functools.partial(fenced, gather)
    inv1[...] = eliminated(a[:BASE, :BASE], work, invb, hooks)
    cross[...] = dot(a[BASE:, :BASE], inv1[...], 1, 1, HIGHEST)
    inv2 = eliminated(a[BASE:, BASE:] - dot(cross[...], cross[...], 1, 1, HIGHEST), work, invb, hooks)

    pa, pb = split(own, 0.53)
    top, low = pl.ds(0, pa), pl.ds(pa, pb)

    def solve(rows):
        right = dot(keep0[rows, BASE:], inv2, 1, 1, HIGHEST)
        solution_rows[rows, BASE:] = right
        pan[0, rows, BASE:] = right.astype(BF16)

    tops = [pl.ds(0, pa // 32 * 16), pl.ds(pa // 32 * 16, pa - pa // 32 * 16)]
    lows = [pl.ds(pa, pb // 32 * 16), pl.ds(pa + pb // 32 * 16, pb - pb // 32 * 16)]
    ends = [y for y in (1, 3) if y < groups // XLO]
    relay = 2 in ys

    def add(o):
        acc[...] += dot(pan[o], big[o], 0, 0)

    def pass_on(kind, y, x, pieces, n):
        if relay:
            mail.start((kind, n), pan.at[2 * y + x, pieces[n]], pan.at[4 + x, pieces[n]], peer[2 * (y ^ 2)])

    def passed(kind, x, pieces):
        for n in range(2):
            mail.take((kind, n), pan.at[4 + x, pieces[n]], peer[2 * ends[1 - n]])

    solve(slice(0, pa))
    for y in ends:
        mail.start(("g2", y), pan.at[0, top], pan.at[2 * y, top], peer[2 * y])
    solve(slice(pa, own))
    mail.start("g1", pan.at[0, low], pan.at[1, low], peer[1])
    mail.start("g3", pan.at[0, top], pan.at[1, top], peer[1])
    for y in ends:
        mail.start(("g4", y), pan.at[0, low], pan.at[2 * y, low], peer[2 * y])
    written = pltpu.make_async_copy(solution_rows, panel, load.at[groups])
    written.start()
    acc[...] = dot(pan[0], big[0], 0, 0)
    for n, y in enumerate(ends):
        mail.take(("g2", y), pan.at[2 * y, top], peer[2 * y])
        pass_on("h2", y, 0, tops, n)
        mail.start(("g6", y), pan.at[2 * y, top], pan.at[2 * y + 1, top], peer[1])
    mail.take("g1", pan.at[1, low], peer[1])
    for y in ends:
        mail.start(("g5", y), pan.at[1, low], pan.at[2 * y + 1, low], peer[2 * y])
    for n, y in enumerate(ends):
        mail.take(("g4", y), pan.at[2 * y, low], peer[2 * y])
        pass_on("h4", y, 0, lows, n)
    mail.take("g3", pan.at[1, top], peer[1])
    add(1)
    if relay:
        passed("h2", 0, tops)
        mail.start(("g6", 2), pan.at[4, top], pan.at[5, top], peer[1])
    for y in ends:
        add(2 * y)
    for n, y in enumerate(ends):
        mail.take(("g5", y), pan.at[2 * y + 1, low], peer[2 * y])
        pass_on("h5", y, 1, lows, n)
    for y in ends:
        mail.take(("g6", y), pan.at[2 * y + 1, top], peer[1])
        add(2 * y + 1)
    if relay:
        passed("h4", 0, lows)
        add(4)
        mail.take(("g6", 2), pan.at[5, top], peer[1])
        passed("h5", 1, lows)
        add(5)

    piece = sums.shape[3]
    scale = 1.0 / math.sqrt(N1)
    halves = [range(0, (depth + 1) // 2), range((depth + 1) // 2, depth)]
    halves = [h for h in halves if len(h)]
    tiles = acc.shape[1] // LANES
    done = 0
    for e in range(tiles):
        turned = jnp.transpose(acc[:, e * LANES : (e + 1) * LANES]) * scale
        for k in range(LANES // piece):
            n = e * (LANES // piece) + k
            zz, xx, cc = n // (XHI * CORES), (n // CORES) % XHI, n % CORES
            sums[cc, zz, xx] = turned[k * piece : (k + 1) * piece, :]
        if done < len(halves) and n + 1 == len(halves[done]) * XHI * CORES + (halves[done][0]) * XHI * CORES:
            part = pl.ds(halves[done][0], len(halves[done]))
            mail.start(("s1", done), sums.at[1 - core, part], core_got.at[part], cpart)
            done += 1
    assert done == len(halves)
    for n, h in enumerate(halves):
        mail.take(("s1", n), core_got.at[pl.ds(h[0], len(h))], cpart)
    value = (sums[core] + core_got[...]).reshape(depth * XHI * piece, width)
    keep1[...] = value.reshape(keep1.shape)
    peak = jnp.maximum(jnp.max(jnp.abs(value), axis=0, keepdims=True), 1e-30)
    z_scale[...] = peak * (1.0 / TOP)
    z_code[...] = jnp.round(value * (TOP / peak)).astype(jnp.int32).astype(I16).reshape(z_code.shape)
    for c in chips:
        mail.start("s2s", z_scale, z_sgot.at[slot[c]], chip[c], z_sgot)
        mail.start("s2", z_code.at[(z + c[0]) % depth, xhi ^ c[1]], z_got.at[slot[c]], chip[c], z_got)
    mail.take("s2s", z_sgot, xpart)
    mail.take("s2", z_got, xpart)
    value = keep1[z, xhi]
    for n in range(len(chips)):
        value = value + decode(z_got[n], z_sgot[n])
    last[...] = value
    finished = pltpu.make_async_copy(last, out, load.at[groups + 1])
    finished.start()
    written.wait()
    mail.close()
    finished.wait()
    assert len(mail.ids) <= send.shape[0], len(mail.ids)


def call(groups, count, border, inverse, prior, sel, asg, prob):
    size = border.shape[1]
    own, width = prior.shape
    depth = count // (CORES * XHI)
    messages = 59
    n = max(depth - 1, 1)
    others = depth * XHI - 1
    piece = size // count
    high = size // LANES * width
    ny = groups // XLO
    ra, rb = split(own, 0.53)
    dma, vmem = pltpu.SemaphoreType.DMA, pltpu.VMEM
    anyspace = pl.BlockSpec(memory_space=pl.ANY)
    return pl.pallas_call(
        functools.partial(kernel, groups, count),
        out_shape=(jax.ShapeDtypeStruct((own, width), F32), jax.ShapeDtypeStruct((piece, width), F32)),
        in_specs=[anyspace] * 6,
        out_specs=(anyspace, anyspace),
        scratch_shapes=[
            vmem((1, width), jnp.int32),
            pltpu.SMEM((groups,), jnp.int32),
            pltpu.SMEM((groups,), F32),
            vmem((piece, width), F32),
            vmem((groups, own, size), BF16),
            vmem((size, size), BF16),
            vmem((own, width), BF16),
            vmem((high, LANES), BF16),
            vmem((high, LANES), BF16),
            vmem((groups, width, own), BF16),
            vmem((high // CORES, LANES), BF16),
            vmem((others, high // count, LANES), BF16),
            vmem((2 * width, LANES), BF16),
            vmem((2 * width // CORES, LANES), BF16),
            vmem((2 * width // (CORES * XHI), LANES), BF16),
            vmem((n, 2 * width // count, LANES), BF16),
            vmem((2 * width // count, LANES), BF16),
            vmem((groups - 1, 2 * width // count, LANES), BF16),
            vmem((2 * width, LANES), BF16),
            vmem((width, size), BF16),
            vmem((size, width), BF16),
            vmem((width // CORES // min(4, depth), width), F32),
            vmem((groups - 1, width // CORES // min(4, depth), width), F32),
            vmem((width, width), F32),
            vmem((ny, 2, ra, width), I16),
            vmem((ny, 2, 1, width), F32),
            vmem((ny, 2, ra, width), I16),
            vmem((ny, 2, 1, width), F32),
            vmem((ny, rb, width), I16),
            vmem((ny, 1, width), F32),
            vmem((ny, rb, width), I16),
            vmem((ny, 1, width), F32),
            vmem((ra, width), I16),
            vmem((1, width), F32),
            vmem((ra, width), I16),
            vmem((1, width), F32),
            vmem((ny, rb, width), I16),
            vmem((ny, 1, width), F32),
            vmem((ny, rb, width), I16),
            vmem((ny, 1, width), F32),
            vmem((own, width), F32),
            vmem((own, width), F32),
            vmem((ra, width), F32),
            vmem((ny, rb, width), F32),
            vmem((own, width), F32),
            vmem((BASE, 2 * BASE), F32),
            vmem((BASE, BASE), F32),
            vmem((BASE, BASE), F32),
            vmem((BASE, BASE), F32),
            vmem((groups, own, width), BF16),
            vmem((width, size), F32),
            vmem((CORES, depth, XHI, piece, width), F32),
            vmem((depth, XHI, piece, width), F32),
            vmem((depth, XHI, piece, width), F32),
            vmem((depth, XHI, piece, width), I16),
            vmem((1, width), F32),
            vmem((others, piece, width), I16),
            vmem((others, 1, width), F32),
            dma((groups + 5,)),
            dma((messages,)),
            dma((messages,)),
        ],
        compiler_params=pltpu.CompilerParams(
            collective_id=0, has_side_effects=True, vmem_limit_bytes=60 << 20
        ),
        name="panel",
    )(border, inverse, prior, sel, asg, prob)


def finish_kernel(panel, residual, panel_out, residual_out, held, kept, came, went):
    rows = panel.shape[0] // 4
    parts = [(panel.at[pl.ds(n * rows, rows)], held.at[n], panel_out.at[pl.ds(n * rows, rows)]) for n in range(4)]
    parts = [(residual, kept, residual_out)] + parts
    ins = [pltpu.make_async_copy(src, mid, came.at[n]) for n, (src, mid, _) in enumerate(parts)]
    outs = [pltpu.make_async_copy(mid, dst, went.at[n]) for n, (_, mid, dst) in enumerate(parts)]
    for go in ins:
        go.start()
    for go, out in zip(ins, outs):
        go.wait()
        out.start()
    for out in outs:
        out.wait()


def finish(panel, residual):
    anyspace = pl.BlockSpec(memory_space=pl.ANY)
    rows, width = panel.shape
    return pl.pallas_call(
        finish_kernel,
        out_shape=(jax.ShapeDtypeStruct(panel.shape, F32), jax.ShapeDtypeStruct(residual.shape, F32)),
        in_specs=[anyspace, anyspace],
        out_specs=(anyspace, anyspace),
        scratch_shapes=[
            pltpu.VMEM((4, rows // 4, width), F32),
            pltpu.VMEM(residual.shape, F32),
            pltpu.SemaphoreType.DMA((5,)),
            pltpu.SemaphoreType.DMA((5,)),
        ],
        name="finish",
    )(panel, residual)


def body(border, inverse_blocks, selected, assignment, probability, prior_panel):
    groups, count = lax.axis_size("grp"), lax.axis_size("dev")
    panel, residual = call(
        groups, count, border[0], inverse_blocks[0], prior_panel, selected[None, :], assignment, probability
    )
    panel, residual = finish(panel, residual)
    return (panel, residual[None])


def solution(mesh):
    return jax.shard_map(
        body,
        mesh=mesh,
        in_specs=(
            P("grp", "dev", None),
            P("grp", None, None),
            P(),
            P(),
            P(),
            P(("dev", "grp"), None),
        ),
        out_specs=(P(("dev", "grp"), None), P("grp", "dev", None)),
        check_vma=False,
    )
```

```python
import functools
import math

import jax
import jax.numpy as jnp
from jax import lax
from jax.experimental import pallas as pl
from jax.experimental.pallas import tpu as pltpu
from jax.sharding import PartitionSpec as P

N1 = 131072
MESH = pl.DeviceIdType.MESH
HIGHEST = lax.Precision.HIGHEST
F32 = jnp.float32
BF16 = jnp.bfloat16
I16 = jnp.int16
LANES = 128
CORES, XHI, XLO = 2, 2, 2
TOP = 32767.0
BASE, PANEL = 128, 16


def dot(a, b, ca, cb, precision=None):
    return lax.dot_general(
        a, b, (((ca,), (cb,)), ((), ())), precision=precision, preferred_element_type=F32
    )


def split(own, share):
    part = max(16, int(own * share / 16 + 0.5) * 16)
    return own - part, part


def encode(x, code, scale):
    peak = jnp.maximum(jnp.max(jnp.abs(x), axis=0, keepdims=True), 1e-30)
    code[...] = jnp.round(x * (TOP / peak)).astype(jnp.int32).astype(I16)
    scale[...] = peak * (1.0 / TOP)


def decode(code, scale):
    return code.astype(jnp.int32).astype(F32) * scale


def eliminate(work, inv, hooks):
    size = work.shape[0]
    shape = (PANEL, size)
    row = lax.broadcasted_iota(jnp.int32, shape, 0)
    spread = lambda x: jnp.broadcast_to(x, shape)
    left, right = slice(0, size), slice(size, 2 * size)
    for at in range(0, size, PANEL):
        here = slice(at, at + PANEL)
        block, side = work[here, left], work[here, right]
        cs = [spread(block[:, at + j : at + j + 1]) for j in range(PANEL)]
        pivots = jnp.zeros(shape, F32)
        for j in range(PANEL):
            pivots = jnp.where(row == j, cs[j], pivots)
            m = jnp.where(row > j, cs[j] * spread(1.0 / cs[j][j : j + 1, :]), 0.0)
            for k in range(j + 1, PANEL):
                cs[k] = cs[k] - m * spread(cs[k][j : j + 1, :])
            block = block - m * spread(block[j : j + 1, :])
            side = side - m * spread(side[j : j + 1, :])
        r = lax.rsqrt(pivots)
        r = r * (1.5 - 0.5 * pivots * r * r)
        block, side = block * r, side * r
        inv[here, :] = side
        turned = jnp.transpose(block)
        if at + PANEL < size:
            there = slice(at + PANEL, at + 2 * PANEL)
            a, b = work[there, left], work[there, right]
            for j in range(PANEL):
                t = spread(turned[there, j : j + 1])
                a = a - t * spread(block[j : j + 1, :])
                b = b - t * spread(side[j : j + 1, :])
            work[there, left] = a
            work[there, right] = b
        if at + 2 * PANEL < size:
            there = slice(at + 2 * PANEL, size)
            update = dot(block, jnp.concatenate([block, side], axis=1), 0, 0, HIGHEST)
            work[there, :] = work[there, :] - update[there, :]
        hooks.pop(0)()


def eliminated(a, work, inv, hooks):
    n = a.shape[0]
    i = lax.broadcasted_iota(jnp.int32, (n, n), 0)
    j = lax.broadcasted_iota(jnp.int32, (n, n), 1)
    work[...] = jnp.concatenate([a, (i == j).astype(F32)], axis=1)
    eliminate(work, inv, hooks)
    return inv[...]


class Mail:
    LOT = 3072 * 2 * LANES

    def __init__(self, send, recv, spare, spare_scales):
        self.send, self.recv, self.spare, self.spare_scales = send, recv, spare, spare_scales
        self.ids, self.lots, self.scales = {}, [0], 0

    def copy(self, key, src, dst, where, lot=0):
        k = self.ids.setdefault(key, len(self.ids))
        return pltpu.make_async_remote_copy(
            src_ref=src, dst_ref=dst, send_sem=self.send.at[lot], recv_sem=self.recv.at[k],
            device_id=where, device_id_type=MESH,
        )

    def start(self, key, src, dst, where):
        shape = src.shape
        if src.dtype == F32 and shape[-2] == 1:
            self.scales += math.prod(shape[:-2])
            lot = 0
        else:
            size = math.prod(shape) * jnp.dtype(src.dtype).itemsize
            if self.lots[-1] + size > self.LOT:
                self.lots.append(0)
            self.lots[-1] += size
            lot = len(self.lots)
        self.copy(key, src, dst, where, lot).start()

    def take(self, key, dst, where):
        self.copy(key, dst, dst, where).wait_recv()

    def close(self, where):
        if self.scales:
            ref = self.spare_scales.at[pl.ds(0, self.scales)]
            self.copy("r1", ref, ref, where).wait_send()
        for n, size in enumerate(self.lots):
            ref = self.spare.at[pl.ds(0, size // (2 * LANES))]
            self.copy("r1", ref, ref, where, n + 1).wait_send()
        assert len(self.ids) <= self.recv.shape[0] and len(self.lots) < self.send.shape[0]


def kernel(
    groups, count, border, inverse, prior_hbm, sel_hbm, asg_hbm, prob_hbm, panel, out,
    sel, asg, prob, last, big, minv, prior, flat, rows, hot, got1, got2, q0, qh, qx, qz, qv, qg, q, picked, project,
    corner, corner_got, corner_sum, ya, ya_s, ya_g, ya_sg, xb, xb_s, xb_g, xb_sg,
    xa, xa_s, xa_g, xa_sg, yb, yb_s, yb_g, yb_sg, keep0, solution_rows, keep_a, keep_b, hit, work, invb, inv1, cross,
    pan, acc, sums, core_got, keep1, z_code, z_scale, z_got, z_sgot,
    spare, spare_scales, load, send, recv,
):
    grp, dev = lax.axis_index("grp"), lax.axis_index("dev")
    depth = count // (CORES * XHI)
    z, xhi, core = dev // (CORES * XHI), (dev // CORES) % XHI, dev % CORES
    at = lambda zz, xx, cc: (grp, (zz * XHI + xx) * CORES + cc)
    cpart, xpart = at(z, xhi, 1 - core), at(z, 1 - xhi, core)
    zparts = {o: at((z + o) % depth, xhi, core) for o in range(1, depth)}
    far = sorted(range(depth), key=lambda o: -min(o, depth - o))
    chips = [(o, x) for o in far for x in (1, 0) if (o, x) != (0, 0)]
    chip = {c: at((z + c[0]) % depth, xhi ^ c[1], core) for c in chips}
    slot = {c: i for i, c in enumerate(chips)}
    ys = [y for y in (2, 1, 3) if y < groups // XLO]
    near = [o for o in (5, 4, 7, 6, 3, 2, 1) if o < groups]
    peer = {o: (grp ^ o, dev) for o in near}
    width, size = picked.shape
    own = prior.shape[0]
    mail = Mail(send, recv, spare, spare_scales)

    def fenced(f, *args):
        pl.when(grp >= 0)(functools.partial(f, *args))

    loads = {o: pltpu.make_async_copy(border.at[pl.ds((grp ^ o) * own, own)], big.at[o], load.at[o]) for o in range(groups)}
    loads["prior"] = pltpu.make_async_copy(prior_hbm, prior, load.at[groups])
    loads["inverse"] = pltpu.make_async_copy(inverse, minv, load.at[groups + 1])
    loads["sel"] = pltpu.make_async_copy(sel_hbm, sel, load.at[groups + 2])
    loads["asg"] = pltpu.make_async_copy(asg_hbm, asg, load.at[groups + 3])
    loads["prob"] = pltpu.make_async_copy(prob_hbm, prob, load.at[groups + 4])
    for name in ["sel"] + list(range(groups)) + ["prior", "inverse", "asg", "prob"]:
        loads[name].start()
    barrier = pltpu.get_barrier_semaphore()
    partners = [cpart] + list(chip.values()) + list(peer.values())
    for where in partners:
        pl.semaphore_signal(barrier, inc=1, device_id=where, device_id_type=MESH)

    loads["sel"].wait()
    want = jnp.transpose(jnp.broadcast_to(sel[...], (LANES, width)))[:, :1]
    want = jnp.broadcast_to(want, (width, own))
    lanes = lax.broadcasted_iota(jnp.int32, (width, own), 1)
    first = (dev * groups + grp) * own
    high = flat.shape[0]
    half, quarter, bit = high // CORES, high // (CORES * XHI), high // count
    at1 = core * half
    part = size // CORES

    def pick(which):
        total = None
        at = pl.multiple_of(which * part, LANES)
        for o in range(groups):
            if which is not core:
                loads[o].wait()
                base = (dev * groups + (grp ^ o)) * own
                hot[o] = (want - base == lanes).astype(F32).astype(BF16)
            got = dot(hot[o], big[o, :, pl.ds(at, part)], 1, 0)
            total = got if total is None else total + got
        total = total.astype(BF16)
        for c in range(part // LANES):
            flat[pl.ds(which * half + c * width, width), :] = total[:, c * LANES : (c + 1) * LANES]

    pick(1 - core)
    pl.semaphore_wait(barrier, len(partners))
    fenced(lambda: mail.start("r1", flat.at[pl.ds((1 - core) * half, half)], got1, cpart))
    pick(core)
    loads["prior"].wait()
    mine = dot((want - first == lanes).astype(F32).astype(BF16), prior[...], 1, 0).astype(BF16)
    for c in range(2):
        q0[pl.ds(c * width, width), :] = mine[:, c * LANES : (c + 1) * LANES]

    qhalf, qquart, qbit = 2 * width // CORES, 2 * width // (CORES * XHI), 2 * width // count
    at3 = at1 + xhi * quarter + z * bit
    qat1 = core * qhalf
    qat2 = qat1 + xhi * qquart
    qat3 = qat2 + z * qbit
    mail.start("q1", q0.at[pl.ds((1 - core) * qhalf, qhalf)], qh, cpart)
    mail.take("r1", got1, cpart)
    flat[pl.ds(at1, half), :] = flat[pl.ds(at1, half), :] + got1[...]
    for c in chips:
        there = at1 + (xhi ^ c[1]) * quarter + ((z + c[0]) % depth) * bit
        mail.start("r2", flat.at[pl.ds(there, bit)], got2.at[slot[c]], chip[c])
    mail.take("q1", qh, cpart)
    q0[pl.ds(qat1, qhalf), :] = q0[pl.ds(qat1, qhalf), :] + qh[...]
    mail.start("q2", q0.at[pl.ds(qat1 + (1 - xhi) * qquart, qquart)], qx, xpart)
    ids = first + lax.broadcasted_iota(jnp.int32, (own, width), 0)
    marked = jnp.max((ids == sel[...]).astype(F32), axis=1, keepdims=True)
    hit[...] = jnp.broadcast_to(marked, hit.shape)
    mail.take("q2", qx, xpart)
    q0[pl.ds(qat2, qquart), :] = q0[pl.ds(qat2, qquart), :] + qx[...]
    for o in zparts:
        mail.start("q3", q0.at[pl.ds(qat2 + ((z + o) % depth) * qbit, qbit)], qz.at[o - 1], zparts[o])
    mail.take("r2", got2, xpart)
    value = flat[pl.ds(at3, bit), :]
    for c in chips:
        value = value + got2[slot[c]]
    rows[pl.ds(at3, bit), :] = value
    here = rows.at[pl.ds(at3, bit)]
    rings = [chips[i : i + 5] for i in range(0, len(chips), 5)]
    for n, ring in enumerate(rings):
        for c in ring:
            mail.start(("r3", n), here, here, chip[c])
    other = rows.at[pl.ds((1 - core) * half, half)]
    mail.start("r4", here, here, cpart)
    value = q0[pl.ds(qat3, qbit), :]
    if zparts:
        mail.take("q3", qz, xpart)
    for o in zparts:
        value = value + qz[o - 1]
    qv[...] = value
    for n, o in enumerate(near):
        mail.start("q4", qv, qg.at[n], peer[o])

    def forward(n):
        mail.take(("r3", n), got2.at[pl.ds(0, len(rings[n]))], xpart)
        for c in rings[n]:
            there = rows.at[pl.ds(at1 + (xhi ^ c[1]) * quarter + ((z + depth - c[0]) % depth) * bit, bit)]
            mail.start("r4", there, there, cpart)

    order = list(range(len(rings)))[::-1]
    forward(order[0])
    mail.take("q4", qg, xpart)
    value = qv[...]
    for n in range(len(near)):
        value = value + qg[n]
    q[pl.ds(qat3, qbit), :] = value
    here = q.at[pl.ds(qat3, qbit)]
    mail.start("q5", here, here, xpart)
    for n in order[1:]:
        forward(n)
    mail.take("r4", other, cpart)

    for c in range(size // LANES):
        picked[:, c * LANES : (c + 1) * LANES] = rows[pl.ds(c * width, width), :]
    loads["inverse"].wait()
    project[...] = dot(minv[...], picked[...], 1, 1).astype(BF16)
    loads["asg"].wait()
    loads["prob"].wait()
    scenario = asg[grp]
    weight = 0.0
    for i in range(groups):
        weight = weight + jnp.where(scenario == i, prob[i], 0.0)
    turn = min(4, depth)
    steps = {4: (2, 1, depth - 1), 2: (1,), 1: ()}[turn]
    chalf, cpiece = width // CORES, width // CORES // turn
    cmine = pl.ds(core * chalf + z % turn * cpiece, cpiece)
    corner[...] = weight * dot(picked[cmine, :], project[...], 1, 0)
    for n, o in enumerate(near):
        mail.start("c1", corner, corner_got.at[n], peer[o])
    ra, rb = split(own, 0.53)

    def block(o):
        return weight * jnp.dot(big[o], project[...], preferred_element_type=F32)

    def make(y):
        side = block(2 * y + 1)
        encode(side[ra:], xb.at[y], xb_s.at[y])
        if y:
            encode(side[:ra], ya.at[y, 1], ya_s.at[y, 1])
            same = block(2 * y)
            encode(same[:ra], ya.at[y, 0], ya_s.at[y, 0])
            keep_b[y] = same[ra:]
        else:
            keep_a[...] = side[:ra]

    def ship(y):
        mail.start(("xbs", y), xb_s.at[y], xb_sg.at[y], peer[1])
        mail.start(("xb", y), xb.at[y], xb_g.at[y], peer[1])
        if y:
            mail.start(("yas", y), ya_s.at[y], ya_sg.at[y], peer[2 * y])
            mail.start(("ya", y), ya.at[y], ya_g.at[y], peer[2 * y])

    lots = q.at[pl.ds(0, XHI * (depth - 1) * qbit)]
    rest = corner_sum.at[pl.ds(0, (turn - 1) * cpiece)]

    def blocks(y):
        make(y)
        ship(y)

    def corner_out():
        mail.take("c1", corner_got, xpart)
        value = corner[...]
        for n in range(len(near)):
            value = value + corner_got[n]
        corner_sum[cmine, :] = value
        here = corner_sum.at[cmine]
        for o in steps:
            mail.start("c2", here, here, zparts[o])
        mail.start("c3", here, here, cpart)

    def prior_out():
        mail.take("q5", q.at[pl.ds(qat1 + (1 - xhi) * qquart + z * qbit, qbit)], xpart)
        for o in zparts:
            for x in range(XHI):
                here = q.at[pl.ds(qat1 + x * qquart + z * qbit, qbit)]
                mail.start("q6", here, here, zparts[o])

    def prior_over():
        if zparts:
            mail.take("q6", lots, xpart)
        here = q.at[pl.ds(qat1, qhalf)]
        mail.start("q7", here, here, cpart)

    for y in ys[:1]:
        fenced(blocks, y)
    fenced(prior_out)
    for y in ys[1:2]:
        fenced(blocks, y)
    fenced(corner_out)
    for y in ys[2:] + [0]:
        fenced(blocks, y)
    fenced(prior_over)
    keep0[...] = block(0)
    mail.take("q7", q.at[pl.ds((1 - core) * qhalf, qhalf)], cpart)
    picks = jnp.concatenate([q[pl.ds(c * width, width), :] for c in range(2)], axis=1)
    keep0[...] -= dot(prior[...], picks, 1, 1)
    less = dot(picks, picks, 1, 1)
    if zparts:
        mail.take("c2", rest, xpart)
    for o in range(1, turn):
        here = corner_sum.at[pl.ds(core * chalf + (z + o) % turn * cpiece, cpiece)]
        mail.start("c3", here, here, cpart)
    mail.take("c3", corner_sum.at[pl.ds((1 - core) * chalf, chalf)], cpart)
    a = corner_sum[...] - less
    a = 0.5 * (a + jnp.transpose(a))

    def onward(y):
        mail.take(("xbs", y), xb_sg.at[y], peer[1])
        mail.take(("xb", y), xb_g.at[y], peer[1])
        encode(keep_b[y] + decode(xb_g[y], xb_sg[y]), yb.at[y], yb_s.at[y])
        mail.start(("ybs", y), yb_s.at[y], yb_sg.at[y], peer[2 * y])
        mail.start(("yb", y), yb.at[y], yb_g.at[y], peer[2 * y])

    def across():
        value, here = keep_a[...], keep0[:ra, :]
        for y in ys:
            mail.take(("yas", y), ya_sg.at[y], peer[2 * y])
            mail.take(("ya", y), ya_g.at[y], peer[2 * y])
            value = value + decode(ya_g[y, 1], ya_sg[y, 1])
            here = here + decode(ya_g[y, 0], ya_sg[y, 0])
        encode(value, xa, xa_s)
        mail.start("xas", xa_s, xa_sg, peer[1])
        mail.start("xa", xa, xa_g, peer[1])
        keep0[:ra, :] = here

    def gather():
        mail.take("xas", xa_sg, peer[1])
        mail.take("xa", xa_g, peer[1])
        mail.take(("xbs", 0), xb_sg.at[0], peer[1])
        mail.take(("xb", 0), xb_g.at[0], peer[1])
        keep0[:ra, :] = keep0[:ra, :] + decode(xa_g[...], xa_sg[...])
        lower = keep0[ra:, :] + decode(xb_g[0], xb_sg[0])
        for y in ys:
            mail.take(("ybs", y), yb_sg.at[y], peer[2 * y])
            mail.take(("yb", y), yb_g.at[y], peer[2 * y])
            lower = lower + decode(yb_g[y], yb_sg[y])
        keep0[ra:, :] = lower
        whole = jnp.where(hit[...] > 0.5, 0.0, keep0[...])
        left = dot(whole[:, :BASE], inv1[...], 1, 1, HIGHEST)
        solution_rows[:, :BASE] = left
        pan[0, :, :BASE] = left.astype(BF16)
        keep0[:, BASE:] = whole[:, BASE:] - dot(left, cross[...], 1, 1, HIGHEST)

    hooks = [lambda: None for _ in range(width // PANEL)]
    for y, n in zip(ys, (0, 1, 4)):
        hooks[n] = functools.partial(fenced, onward, y)
    hooks[7] = functools.partial(fenced, across)
    hooks[15] = functools.partial(fenced, gather)
    inv1[...] = eliminated(a[:BASE, :BASE], work, invb, hooks)
    cross[...] = dot(a[BASE:, :BASE], inv1[...], 1, 1, HIGHEST)
    inv2 = eliminated(a[BASE:, BASE:] - dot(cross[...], cross[...], 1, 1, HIGHEST), work, invb, hooks)

    pa, pb = split(own, 0.53)
    top, low = pl.ds(0, pa), pl.ds(pa, pb)

    def solve(rows):
        right = dot(keep0[rows, BASE:], inv2, 1, 1, HIGHEST)
        solution_rows[rows, BASE:] = right
        pan[0, rows, BASE:] = right.astype(BF16)

    tops = [pl.ds(0, pa // 32 * 16), pl.ds(pa // 32 * 16, pa - pa // 32 * 16)]
    lows = [pl.ds(pa, pb // 32 * 16), pl.ds(pa + pb // 32 * 16, pb - pb // 32 * 16)]
    ends = [y for y in (1, 3) if y < groups // XLO]
    relay = 2 in ys

    def add(o):
        acc[...] += dot(pan[o], big[o], 0, 0)

    def pass_on(kind, y, x, pieces, n):
        if relay:
            mail.start((kind, n), pan.at[2 * y + x, pieces[n]], pan.at[4 + x, pieces[n]], peer[2 * (y ^ 2)])

    def passed(kind, x, pieces):
        for n in range(2):
            mail.take((kind, n), pan.at[4 + x, pieces[n]], peer[2 * ends[1 - n]])

    solve(slice(0, pa))
    for y in ends:
        mail.start(("g2", y), pan.at[0, top], pan.at[2 * y, top], peer[2 * y])
    solve(slice(pa, own))
    mail.start("g1", pan.at[0, low], pan.at[1, low], peer[1])
    mail.start("g3", pan.at[0, top], pan.at[1, top], peer[1])
    for y in ends:
        mail.start(("g4", y), pan.at[0, low], pan.at[2 * y, low], peer[2 * y])
    written = pltpu.make_async_copy(solution_rows, panel, load.at[groups])
    written.start()
    acc[...] = dot(pan[0], big[0], 0, 0)
    for n, y in enumerate(ends):
        mail.take(("g2", y), pan.at[2 * y, top], peer[2 * y])
        pass_on("h2", y, 0, tops, n)
        mail.start(("g6", y), pan.at[2 * y, top], pan.at[2 * y + 1, top], peer[1])
    mail.take("g1", pan.at[1, low], peer[1])
    for y in ends:
        mail.start(("g5", y), pan.at[1, low], pan.at[2 * y + 1, low], peer[2 * y])
    for n, y in enumerate(ends):
        mail.take(("g4", y), pan.at[2 * y, low], peer[2 * y])
        pass_on("h4", y, 0, lows, n)
    mail.take("g3", pan.at[1, top], peer[1])
    add(1)
    if relay:
        passed("h2", 0, tops)
        mail.start(("g6", 2), pan.at[4, top], pan.at[5, top], peer[1])
    for y in ends:
        add(2 * y)
    for n, y in enumerate(ends):
        mail.take(("g5", y), pan.at[2 * y + 1, low], peer[2 * y])
        pass_on("h5", y, 1, lows, n)
    for y in ends:
        mail.take(("g6", y), pan.at[2 * y + 1, top], peer[1])
        add(2 * y + 1)
    if relay:
        passed("h4", 0, lows)
        add(4)
        mail.take(("g6", 2), pan.at[5, top], peer[1])
        passed("h5", 1, lows)
        add(5)

    piece = sums.shape[3]
    scale = 1.0 / math.sqrt(N1)
    halves = [range(0, (depth + 1) // 2), range((depth + 1) // 2, depth)]
    halves = [h for h in halves if len(h)]
    tiles = acc.shape[1] // LANES
    done = 0
    for e in range(tiles):
        turned = jnp.transpose(acc[:, e * LANES : (e + 1) * LANES]) * scale
        for k in range(LANES // piece):
            n = e * (LANES // piece) + k
            zz, xx, cc = n // (XHI * CORES), (n // CORES) % XHI, n % CORES
            sums[cc, zz, xx] = turned[k * piece : (k + 1) * piece, :]
        if done < len(halves) and n + 1 == len(halves[done]) * XHI * CORES + (halves[done][0]) * XHI * CORES:
            part = pl.ds(halves[done][0], len(halves[done]))
            mail.start(("s1", done), sums.at[1 - core, part], core_got.at[part], cpart)
            done += 1
    assert done == len(halves)
    for n, h in enumerate(halves):
        mail.take(("s1", n), core_got.at[pl.ds(h[0], len(h))], cpart)
    value = (sums[core] + core_got[...]).reshape(depth * XHI * piece, width)
    keep1[...] = value.reshape(keep1.shape)
    peak = jnp.maximum(jnp.max(jnp.abs(value), axis=0, keepdims=True), 1e-30)
    z_scale[...] = peak * (1.0 / TOP)
    z_code[...] = jnp.round(value * (TOP / peak)).astype(jnp.int32).astype(I16).reshape(z_code.shape)
    for c in chips:
        mail.start("s2s", z_scale, z_sgot.at[slot[c]], chip[c])
        mail.start("s2", z_code.at[(z + c[0]) % depth, xhi ^ c[1]], z_got.at[slot[c]], chip[c])
    mail.take("s2s", z_sgot, xpart)
    mail.take("s2", z_got, xpart)
    value = keep1[z, xhi]
    for n in range(len(chips)):
        value = value + decode(z_got[n], z_sgot[n])
    last[...] = value
    finished = pltpu.make_async_copy(last, out, load.at[groups + 1])
    finished.start()
    written.wait()
    mail.close(cpart)
    finished.wait()


def call(groups, count, border, inverse, prior, sel, asg, prob):
    size = border.shape[1]
    own, width = prior.shape
    depth = count // (CORES * XHI)
    messages = 59
    n = max(depth - 1, 1)
    others = depth * XHI - 1
    piece = size // count
    high = size // LANES * width
    ny = groups // XLO
    ra, rb = split(own, 0.53)
    dma, vmem = pltpu.SemaphoreType.DMA, pltpu.VMEM
    anyspace = pl.BlockSpec(memory_space=pl.ANY)
    return pl.pallas_call(
        functools.partial(kernel, groups, count),
        out_shape=(jax.ShapeDtypeStruct((own, width), F32), jax.ShapeDtypeStruct((piece, width), F32)),
        in_specs=[anyspace] * 6,
        out_specs=(anyspace, anyspace),
        scratch_shapes=[
            vmem((1, width), jnp.int32),
            pltpu.SMEM((groups,), jnp.int32),
            pltpu.SMEM((groups,), F32),
            vmem((piece, width), F32),
            vmem((groups, own, size), BF16),
            vmem((size, size), BF16),
            vmem((own, width), BF16),
            vmem((high, LANES), BF16),
            vmem((high, LANES), BF16),
            vmem((groups, width, own), BF16),
            vmem((high // CORES, LANES), BF16),
            vmem((others, high // count, LANES), BF16),
            vmem((2 * width, LANES), BF16),
            vmem((2 * width // CORES, LANES), BF16),
            vmem((2 * width // (CORES * XHI), LANES), BF16),
            vmem((n, 2 * width // count, LANES), BF16),
            vmem((2 * width // count, LANES), BF16),
            vmem((groups - 1, 2 * width // count, LANES), BF16),
            vmem((2 * width, LANES), BF16),
            vmem((width, size), BF16),
            vmem((size, width), BF16),
            vmem((width // CORES // min(4, depth), width), F32),
            vmem((groups - 1, width // CORES // min(4, depth), width), F32),
            vmem((width, width), F32),
            vmem((ny, 2, ra, width), I16),
            vmem((ny, 2, 1, width), F32),
            vmem((ny, 2, ra, width), I16),
            vmem((ny, 2, 1, width), F32),
            vmem((ny, rb, width), I16),
            vmem((ny, 1, width), F32),
            vmem((ny, rb, width), I16),
            vmem((ny, 1, width), F32),
            vmem((ra, width), I16),
            vmem((1, width), F32),
            vmem((ra, width), I16),
            vmem((1, width), F32),
            vmem((ny, rb, width), I16),
            vmem((ny, 1, width), F32),
            vmem((ny, rb, width), I16),
            vmem((ny, 1, width), F32),
            vmem((own, width), F32),
            vmem((own, width), F32),
            vmem((ra, width), F32),
            vmem((ny, rb, width), F32),
            vmem((own, width), F32),
            vmem((BASE, 2 * BASE), F32),
            vmem((BASE, BASE), F32),
            vmem((BASE, BASE), F32),
            vmem((BASE, BASE), F32),
            vmem((groups, own, width), BF16),
            vmem((width, size), F32),
            vmem((CORES, depth, XHI, piece, width), F32),
            vmem((depth, XHI, piece, width), F32),
            vmem((depth, XHI, piece, width), F32),
            vmem((depth, XHI, piece, width), I16),
            vmem((1, width), F32),
            vmem((others, piece, width), I16),
            vmem((others, 1, width), F32),
            vmem((3072, LANES), BF16),
            vmem((64, 1, width), F32),
            dma((groups + 5,)),
            dma((12,)),
            dma((messages,)),
        ],
        compiler_params=pltpu.CompilerParams(
            collective_id=0, has_side_effects=True, vmem_limit_bytes=60 << 20
        ),
        name="panel",
    )(border, inverse, prior, sel, asg, prob)


def finish_kernel(panel, residual, panel_out, residual_out, held, kept, came, went):
    rows = panel.shape[0] // 4
    parts = [(panel.at[pl.ds(n * rows, rows)], held.at[n], panel_out.at[pl.ds(n * rows, rows)]) for n in range(4)]
    parts = [(residual, kept, residual_out)] + parts
    ins = [pltpu.make_async_copy(src, mid, came.at[n]) for n, (src, mid, _) in enumerate(parts)]
    outs = [pltpu.make_async_copy(mid, dst, went.at[n]) for n, (_, mid, dst) in enumerate(parts)]
    for go in ins:
        go.start()
    for go, out in zip(ins, outs):
        go.wait()
        out.start()
    for out in outs:
        out.wait()


def finish(panel, residual):
    anyspace = pl.BlockSpec(memory_space=pl.ANY)
    rows, width = panel.shape
    return pl.pallas_call(
        finish_kernel,
        out_shape=(jax.ShapeDtypeStruct(panel.shape, F32), jax.ShapeDtypeStruct(residual.shape, F32)),
        in_specs=[anyspace, anyspace],
        out_specs=(anyspace, anyspace),
        scratch_shapes=[
            pltpu.VMEM((4, rows // 4, width), F32),
            pltpu.VMEM(residual.shape, F32),
            pltpu.SemaphoreType.DMA((5,)),
            pltpu.SemaphoreType.DMA((5,)),
        ],
        name="finish",
    )(panel, residual)


def body(border, inverse_blocks, selected, assignment, probability, prior_panel):
    groups, count = lax.axis_size("grp"), lax.axis_size("dev")
    panel, residual = call(
        groups, count, border[0], inverse_blocks[0], prior_panel, selected[None, :], assignment, probability
    )
    panel, residual = finish(panel, residual)
    return (panel, residual[None])


def solution(mesh):
    return jax.shard_map(
        body,
        mesh=mesh,
        in_specs=(
            P("grp", "dev", None),
            P("grp", None, None),
            P(),
            P(),
            P(),
            P(("dev", "grp"), None),
        ),
        out_specs=(P(("dev", "grp"), None), P("grp", "dev", None)),
        check_vma=False,
    )
```

```python
import functools
import math

import jax
import jax.numpy as jnp
from jax import lax
from jax.experimental import pallas as pl
from jax.experimental.pallas import tpu as pltpu
from jax.sharding import PartitionSpec as P

N1 = 131072
MESH = pl.DeviceIdType.MESH
HIGHEST = lax.Precision.HIGHEST
F32 = jnp.float32
BF16 = jnp.bfloat16
I16 = jnp.int16
LANES = 128
CORES, XHI, XLO = 2, 2, 2
TOP = 32767.0
BASE, PANEL = 128, 16


def dot(a, b, ca, cb, precision=None):
    return lax.dot_general(
        a, b, (((ca,), (cb,)), ((), ())), precision=precision, preferred_element_type=F32
    )


def split(own, share):
    part = max(16, int(own * share / 16 + 0.5) * 16)
    return own - part, part


def encode(x, code, scale):
    peak = jnp.maximum(jnp.max(jnp.abs(x), axis=0, keepdims=True), 1e-30)
    code[...] = jnp.round(x * (TOP / peak)).astype(jnp.int32).astype(I16)
    scale[...] = peak * (1.0 / TOP)


def decode(code, scale):
    return code.astype(jnp.int32).astype(F32) * scale


def eliminate(work, inv, hooks):
    size = work.shape[0]
    shape = (PANEL, size)
    row = lax.broadcasted_iota(jnp.int32, shape, 0)
    spread = lambda x: jnp.broadcast_to(x, shape)
    left, right = slice(0, size), slice(size, 2 * size)
    for at in range(0, size, PANEL):
        here = slice(at, at + PANEL)
        block, side = work[here, left], work[here, right]
        cs = [spread(block[:, at + j : at + j + 1]) for j in range(PANEL)]
        pivots = jnp.zeros(shape, F32)
        for j in range(PANEL):
            pivots = jnp.where(row == j, cs[j], pivots)
            m = jnp.where(row > j, cs[j] * spread(1.0 / cs[j][j : j + 1, :]), 0.0)
            for k in range(j + 1, PANEL):
                cs[k] = cs[k] - m * spread(cs[k][j : j + 1, :])
            block = block - m * spread(block[j : j + 1, :])
            side = side - m * spread(side[j : j + 1, :])
        r = lax.rsqrt(pivots)
        r = r * (1.5 - 0.5 * pivots * r * r)
        block, side = block * r, side * r
        inv[here, :] = side
        turned = jnp.transpose(block)
        if at + PANEL < size:
            there = slice(at + PANEL, at + 2 * PANEL)
            a, b = work[there, left], work[there, right]
            for j in range(PANEL):
                t = spread(turned[there, j : j + 1])
                a = a - t * spread(block[j : j + 1, :])
                b = b - t * spread(side[j : j + 1, :])
            work[there, left] = a
            work[there, right] = b
        if at + 2 * PANEL < size:
            there = slice(at + 2 * PANEL, size)
            update = dot(block, jnp.concatenate([block, side], axis=1), 0, 0, HIGHEST)
            work[there, :] = work[there, :] - update[there, :]
        hooks.pop(0)()


def eliminated(a, work, inv, hooks):
    n = a.shape[0]
    i = lax.broadcasted_iota(jnp.int32, (n, n), 0)
    j = lax.broadcasted_iota(jnp.int32, (n, n), 1)
    work[...] = jnp.concatenate([a, (i == j).astype(F32)], axis=1)
    eliminate(work, inv, hooks)
    return inv[...]


class Mail:
    LOT = 3072 * 2 * LANES

    def __init__(self, send, recv, spare, spare_scales):
        self.send, self.recv, self.spare, self.spare_scales = send, recv, spare, spare_scales
        self.ids, self.lots, self.scales = {}, [0], 0

    def copy(self, key, src, dst, where, lot=0):
        k = self.ids.setdefault(key, len(self.ids))
        return pltpu.make_async_remote_copy(
            src_ref=src, dst_ref=dst, send_sem=self.send.at[lot], recv_sem=self.recv.at[k],
            device_id=where, device_id_type=MESH,
        )

    def start(self, key, src, dst, where):
        shape = src.shape
        if src.dtype == F32 and shape[-2] == 1:
            self.scales += math.prod(shape[:-2])
            lot = 0
        else:
            size = math.prod(shape) * jnp.dtype(src.dtype).itemsize
            if self.lots[-1] + size > self.LOT:
                self.lots.append(0)
            self.lots[-1] += size
            lot = len(self.lots)
        self.copy(key, src, dst, where, lot).start()

    def take(self, key, dst, where):
        self.copy(key, dst, dst, where).wait_recv()

    def close(self, where):
        if self.scales:
            ref = self.spare_scales.at[pl.ds(0, self.scales)]
            self.copy("r1", ref, ref, where).wait_send()
        for n, size in enumerate(self.lots):
            ref = self.spare.at[pl.ds(0, size // (2 * LANES))]
            self.copy("r1", ref, ref, where, n + 1).wait_send()
        assert len(self.ids) <= self.recv.shape[0] and len(self.lots) < self.send.shape[0]


def kernel(
    groups, count, border, inverse, prior_hbm, sel_hbm, asg_hbm, prob_hbm, panel, out,
    sel, asg, prob, last, big, minv, prior, flat, rows, hot, got1, got2, q0, qh, qx, qz, qv, qg, q, picked, project,
    corner, corner_got, corner_sum, ya, ya_s, ya_g, ya_sg, xb, xb_s, xb_g, xb_sg,
    xa, xa_s, xa_g, xa_sg, yb, yb_s, yb_g, yb_sg, keep0, solution_rows, keep_a, keep_b, hit, work, invb, inv1, cross,
    pan, acc, sums, core_got, keep1, z_code, z_scale, z_got, z_sgot,
    spare, spare_scales, load, send, recv,
):
    grp, dev = lax.axis_index("grp"), lax.axis_index("dev")
    depth = count // (CORES * XHI)
    z, xhi, core = dev // (CORES * XHI), (dev // CORES) % XHI, dev % CORES
    at = lambda zz, xx, cc: (grp, (zz * XHI + xx) * CORES + cc)
    cpart, xpart = at(z, xhi, 1 - core), at(z, 1 - xhi, core)
    zparts = {o: at((z + o) % depth, xhi, core) for o in range(1, depth)}
    far = sorted(range(depth), key=lambda o: -min(o, depth - o))
    chips = [(o, x) for o in far for x in (1, 0) if (o, x) != (0, 0)]
    chip = {c: at((z + c[0]) % depth, xhi ^ c[1], core) for c in chips}
    slot = {c: i for i, c in enumerate(chips)}
    ys = [y for y in (2, 1, 3) if y < groups // XLO]
    near = [o for o in (5, 4, 7, 6, 3, 2, 1) if o < groups]
    peer = {o: (grp ^ o, dev) for o in near}
    width, size = picked.shape
    own = prior.shape[0]
    mail = Mail(send, recv, spare, spare_scales)

    def fenced(f, *args):
        pl.when(grp >= 0)(functools.partial(f, *args))

    loads = {o: pltpu.make_async_copy(border.at[pl.ds((grp ^ o) * own, own)], big.at[o], load.at[o]) for o in range(groups)}
    loads["prior"] = pltpu.make_async_copy(prior_hbm, prior, load.at[groups])
    loads["inverse"] = pltpu.make_async_copy(inverse, minv, load.at[groups + 1])
    loads["sel"] = pltpu.make_async_copy(sel_hbm, sel, load.at[groups + 2])
    loads["asg"] = pltpu.make_async_copy(asg_hbm, asg, load.at[groups + 3])
    loads["prob"] = pltpu.make_async_copy(prob_hbm, prob, load.at[groups + 4])
    for name in ["sel"] + list(range(groups)) + ["prior", "inverse", "asg", "prob"]:
        loads[name].start()
    barrier = pltpu.get_barrier_semaphore()
    partners = [cpart] + list(chip.values()) + list(peer.values())
    for where in partners:
        pl.semaphore_signal(barrier, inc=1, device_id=where, device_id_type=MESH)

    loads["sel"].wait()
    want = jnp.transpose(jnp.broadcast_to(sel[...], (LANES, width)))[:, :1]
    want = jnp.broadcast_to(want, (width, own))
    lanes = lax.broadcasted_iota(jnp.int32, (width, own), 1)
    first = (dev * groups + grp) * own
    high = flat.shape[0]
    half, quarter, bit = high // CORES, high // (CORES * XHI), high // count
    at1 = core * half
    part = size // CORES

    def pick(which):
        total = None
        at = pl.multiple_of(which * part, LANES)
        for o in range(groups):
            if which is not core:
                loads[o].wait()
                base = (dev * groups + (grp ^ o)) * own
                hot[o] = (want - base == lanes).astype(F32).astype(BF16)
            got = dot(hot[o], big[o, :, pl.ds(at, part)], 1, 0)
            total = got if total is None else total + got
        total = total.astype(BF16)
        for c in range(part // LANES):
            flat[pl.ds(which * half + c * width, width), :] = total[:, c * LANES : (c + 1) * LANES]

    pick(1 - core)
    pl.semaphore_wait(barrier, len(partners))
    fenced(lambda: mail.start("r1", flat.at[pl.ds((1 - core) * half, half)], got1, cpart))
    pick(core)
    loads["prior"].wait()
    mine = dot((want - first == lanes).astype(F32).astype(BF16), prior[...], 1, 0).astype(BF16)
    for c in range(2):
        q0[pl.ds(c * width, width), :] = mine[:, c * LANES : (c + 1) * LANES]

    qhalf, qquart, qbit = 2 * width // CORES, 2 * width // (CORES * XHI), 2 * width // count
    at3 = at1 + xhi * quarter + z * bit
    qat1 = core * qhalf
    qat2 = qat1 + xhi * qquart
    qat3 = qat2 + z * qbit
    mail.start("q1", q0.at[pl.ds((1 - core) * qhalf, qhalf)], qh, cpart)
    mail.take("r1", got1, cpart)
    flat[pl.ds(at1, half), :] = flat[pl.ds(at1, half), :] + got1[...]
    for c in chips:
        there = at1 + (xhi ^ c[1]) * quarter + ((z + c[0]) % depth) * bit
        mail.start("r2", flat.at[pl.ds(there, bit)], got2.at[slot[c]], chip[c])
    mail.take("q1", qh, cpart)
    q0[pl.ds(qat1, qhalf), :] = q0[pl.ds(qat1, qhalf), :] + qh[...]
    mail.start("q2", q0.at[pl.ds(qat1 + (1 - xhi) * qquart, qquart)], qx, xpart)
    ids = first + lax.broadcasted_iota(jnp.int32, (own, width), 0)
    marked = jnp.max((ids == sel[...]).astype(F32), axis=1, keepdims=True)
    hit[...] = jnp.broadcast_to(marked, hit.shape)
    mail.take("q2", qx, xpart)
    q0[pl.ds(qat2, qquart), :] = q0[pl.ds(qat2, qquart), :] + qx[...]
    for o in zparts:
        mail.start("q3", q0.at[pl.ds(qat2 + ((z + o) % depth) * qbit, qbit)], qz.at[o - 1], zparts[o])
    mail.take("r2", got2, xpart)
    value = flat[pl.ds(at3, bit), :]
    for c in chips:
        value = value + got2[slot[c]]
    rows[pl.ds(at3, bit), :] = value
    here = rows.at[pl.ds(at3, bit)]
    rings = [chips[i : i + 5] for i in range(0, len(chips), 5)]
    for n, ring in enumerate(rings):
        for c in ring:
            mail.start(("r3", n), here, here, chip[c])
    other = rows.at[pl.ds((1 - core) * half, half)]
    mail.start("r4", here, here, cpart)
    value = q0[pl.ds(qat3, qbit), :]
    if zparts:
        mail.take("q3", qz, xpart)
    for o in zparts:
        value = value + qz[o - 1]
    qv[...] = value
    for n, o in enumerate(near):
        mail.start("q4", qv, qg.at[n], peer[o])

    def forward(n):
        mail.take(("r3", n), got2.at[pl.ds(0, len(rings[n]))], xpart)
        for c in rings[n]:
            there = rows.at[pl.ds(at1 + (xhi ^ c[1]) * quarter + ((z + depth - c[0]) % depth) * bit, bit)]
            mail.start("r4", there, there, cpart)

    order = list(range(len(rings)))[::-1]
    forward(order[0])
    mail.take("q4", qg, xpart)
    value = qv[...]
    for n in range(len(near)):
        value = value + qg[n]
    q[pl.ds(qat3, qbit), :] = value
    here = q.at[pl.ds(qat3, qbit)]
    mail.start("q5", here, here, xpart)
    for n in order[1:]:
        forward(n)
    mail.take("r4", other, cpart)

    for c in range(size // LANES):
        picked[:, c * LANES : (c + 1) * LANES] = rows[pl.ds(c * width, width), :]
    loads["inverse"].wait()
    project[...] = dot(minv[...], picked[...], 1, 1).astype(BF16)
    loads["asg"].wait()
    loads["prob"].wait()
    scenario = asg[grp]
    weight = 0.0
    for i in range(groups):
        weight = weight + jnp.where(scenario == i, prob[i], 0.0)
    turn = min(4, depth)
    steps = {4: (2, 1, depth - 1), 2: (1,), 1: ()}[turn]
    chalf, cpiece = width // CORES, width // CORES // turn
    cmine = pl.ds(core * chalf + z % turn * cpiece, cpiece)
    corner[...] = weight * dot(picked[cmine, :], project[...], 1, 0)
    for n, o in enumerate(near):
        mail.start("c1", corner, corner_got.at[n], peer[o])
    ra, rb = split(own, 0.53)

    def block(o):
        return weight * jnp.dot(big[o], project[...], preferred_element_type=F32)

    def make(y):
        side = block(2 * y + 1)
        encode(side[ra:], xb.at[y], xb_s.at[y])
        if y:
            encode(side[:ra], ya.at[y, 1], ya_s.at[y, 1])
            same = block(2 * y)
            encode(same[:ra], ya.at[y, 0], ya_s.at[y, 0])
            keep_b[y] = same[ra:]
        else:
            keep_a[...] = side[:ra]

    def ship(y):
        mail.start(("xbs", y), xb_s.at[y], xb_sg.at[y], peer[1])
        mail.start(("xb", y), xb.at[y], xb_g.at[y], peer[1])
        if y:
            mail.start(("yas", y), ya_s.at[y], ya_sg.at[y], peer[2 * y])
            mail.start(("ya", y), ya.at[y], ya_g.at[y], peer[2 * y])

    lots = q.at[pl.ds(0, XHI * (depth - 1) * qbit)]
    rest = corner_sum.at[pl.ds(0, (turn - 1) * cpiece)]

    def blocks(y):
        make(y)
        ship(y)

    def corner_out():
        mail.take("c1", corner_got, xpart)
        value = corner[...]
        for n in range(len(near)):
            value = value + corner_got[n]
        corner_sum[cmine, :] = value
        here = corner_sum.at[cmine]
        for o in steps:
            mail.start("c2", here, here, zparts[o])
        mail.start("c3", here, here, cpart)

    def prior_out():
        mail.take("q5", q.at[pl.ds(qat1 + (1 - xhi) * qquart + z * qbit, qbit)], xpart)
        for o in zparts:
            for x in range(XHI):
                here = q.at[pl.ds(qat1 + x * qquart + z * qbit, qbit)]
                mail.start("q6", here, here, zparts[o])

    def prior_over():
        if zparts:
            mail.take("q6", lots, xpart)
        here = q.at[pl.ds(qat1, qhalf)]
        mail.start("q7", here, here, cpart)

    for y in ys[:1]:
        fenced(blocks, y)
    fenced(prior_out)
    for y in ys[1:2]:
        fenced(blocks, y)
    fenced(corner_out)
    for y in ys[2:] + [0]:
        fenced(blocks, y)
    fenced(prior_over)
    keep0[...] = block(0)
    mail.take("q7", q.at[pl.ds((1 - core) * qhalf, qhalf)], cpart)
    picks = jnp.concatenate([q[pl.ds(c * width, width), :] for c in range(2)], axis=1)
    keep0[...] -= dot(prior[...], picks, 1, 1)
    less = dot(picks, picks, 1, 1)
    if zparts:
        mail.take("c2", rest, xpart)
    for o in range(1, turn):
        here = corner_sum.at[pl.ds(core * chalf + (z + o) % turn * cpiece, cpiece)]
        mail.start("c3", here, here, cpart)
    mail.take("c3", corner_sum.at[pl.ds((1 - core) * chalf, chalf)], cpart)
    a = corner_sum[...] - less
    a = 0.5 * (a + jnp.transpose(a))

    def onward(y):
        mail.take(("xbs", y), xb_sg.at[y], peer[1])
        mail.take(("xb", y), xb_g.at[y], peer[1])
        encode(keep_b[y] + decode(xb_g[y], xb_sg[y]), yb.at[y], yb_s.at[y])
        mail.start(("ybs", y), yb_s.at[y], yb_sg.at[y], peer[2 * y])
        mail.start(("yb", y), yb.at[y], yb_g.at[y], peer[2 * y])

    def across():
        value, here = keep_a[...], keep0[:ra, :]
        for y in ys:
            mail.take(("yas", y), ya_sg.at[y], peer[2 * y])
            mail.take(("ya", y), ya_g.at[y], peer[2 * y])
            value = value + decode(ya_g[y, 1], ya_sg[y, 1])
            here = here + decode(ya_g[y, 0], ya_sg[y, 0])
        encode(value, xa, xa_s)
        mail.start("xas", xa_s, xa_sg, peer[1])
        mail.start("xa", xa, xa_g, peer[1])
        keep0[:ra, :] = here

    def gather():
        mail.take("xas", xa_sg, peer[1])
        mail.take("xa", xa_g, peer[1])
        mail.take(("xbs", 0), xb_sg.at[0], peer[1])
        mail.take(("xb", 0), xb_g.at[0], peer[1])
        keep0[:ra, :] = keep0[:ra, :] + decode(xa_g[...], xa_sg[...])
        lower = keep0[ra:, :] + decode(xb_g[0], xb_sg[0])
        for y in ys:
            mail.take(("ybs", y), yb_sg.at[y], peer[2 * y])
            mail.take(("yb", y), yb_g.at[y], peer[2 * y])
            lower = lower + decode(yb_g[y], yb_sg[y])
        keep0[ra:, :] = lower
        whole = jnp.where(hit[...] > 0.5, 0.0, keep0[...])
        left = dot(whole[:, :BASE], inv1[...], 1, 1, HIGHEST)
        solution_rows[:, :BASE] = left
        pan[0, :, :BASE] = left.astype(BF16)
        keep0[:, BASE:] = whole[:, BASE:] - dot(left, cross[...], 1, 1, HIGHEST)

    hooks = [lambda: None for _ in range(width // PANEL)]
    for y, n in zip(ys, (0, 1, 4)):
        hooks[n] = functools.partial(fenced, onward, y)
    hooks[7] = functools.partial(fenced, across)
    hooks[15] = functools.partial(fenced, gather)
    inv1[...] = eliminated(a[:BASE, :BASE], work, invb, hooks)
    cross[...] = dot(a[BASE:, :BASE], inv1[...], 1, 1, HIGHEST)
    inv2 = eliminated(a[BASE:, BASE:] - dot(cross[...], cross[...], 1, 1, HIGHEST), work, invb, hooks)

    pa, pb = split(own, 0.53)
    top, low = pl.ds(0, pa), pl.ds(pa, pb)

    def solve(rows):
        right = dot(keep0[rows, BASE:], inv2, 1, 1, HIGHEST)
        solution_rows[rows, BASE:] = right
        pan[0, rows, BASE:] = right.astype(BF16)

    tops = [pl.ds(0, pa // 32 * 16), pl.ds(pa // 32 * 16, pa - pa // 32 * 16)]
    lows = [pl.ds(pa, pb // 32 * 16), pl.ds(pa + pb // 32 * 16, pb - pb // 32 * 16)]
    ends = [y for y in (1, 3) if y < groups // XLO]
    relay = 2 in ys

    def add(o):
        acc[...] += dot(pan[o], big[o], 0, 0)

    def pass_on(kind, y, x, pieces, n):
        if relay:
            mail.start((kind, n), pan.at[2 * y + x, pieces[n]], pan.at[4 + x, pieces[n]], peer[2 * (y ^ 2)])

    def passed(kind, x, pieces):
        for n in range(2):
            mail.take((kind, n), pan.at[4 + x, pieces[n]], peer[2 * ends[1 - n]])

    solve(slice(0, pa))
    for y in ends:
        mail.start(("g2", y), pan.at[0, top], pan.at[2 * y, top], peer[2 * y])
    solve(slice(pa, own))
    mail.start("g1", pan.at[0, low], pan.at[1, low], peer[1])
    mail.start("g3", pan.at[0, top], pan.at[1, top], peer[1])
    for y in ends:
        mail.start(("g4", y), pan.at[0, low], pan.at[2 * y, low], peer[2 * y])
    written = pltpu.make_async_copy(solution_rows, panel, load.at[groups])
    written.start()
    acc[...] = dot(pan[0], big[0], 0, 0)
    for n, y in enumerate(ends):
        mail.take(("g2", y), pan.at[2 * y, top], peer[2 * y])
        pass_on("h2", y, 0, tops, n)
        mail.start(("g6", y), pan.at[2 * y, top], pan.at[2 * y + 1, top], peer[1])
    mail.take("g1", pan.at[1, low], peer[1])
    for y in ends:
        mail.start(("g5", y), pan.at[1, low], pan.at[2 * y + 1, low], peer[2 * y])
    for n, y in enumerate(ends):
        mail.take(("g4", y), pan.at[2 * y, low], peer[2 * y])
        pass_on("h4", y, 0, lows, n)
    mail.take("g3", pan.at[1, top], peer[1])
    add(1)
    if relay:
        passed("h2", 0, tops)
        mail.start(("g6", 2), pan.at[4, top], pan.at[5, top], peer[1])
    for y in ends:
        add(2 * y)
    for n, y in enumerate(ends):
        mail.take(("g5", y), pan.at[2 * y + 1, low], peer[2 * y])
        pass_on("h5", y, 1, lows, n)
    for y in ends:
        mail.take(("g6", y), pan.at[2 * y + 1, top], peer[1])
        add(2 * y + 1)
    if relay:
        passed("h4", 0, lows)
        add(4)
        mail.take(("g6", 2), pan.at[5, top], peer[1])
        passed("h5", 1, lows)
        add(5)

    piece = sums.shape[3]
    scale = 1.0 / math.sqrt(N1)
    halves = [range(0, (depth + 1) // 2), range((depth + 1) // 2, depth)]
    halves = [h for h in halves if len(h)]
    tiles = acc.shape[1] // LANES
    done = 0
    for e in range(tiles):
        turned = jnp.transpose(acc[:, e * LANES : (e + 1) * LANES]) * scale
        for k in range(LANES // piece):
            n = e * (LANES // piece) + k
            zz, xx, cc = n // (XHI * CORES), (n // CORES) % XHI, n % CORES
            sums[cc, zz, xx] = turned[k * piece : (k + 1) * piece, :]
        if done < len(halves) and n + 1 == len(halves[done]) * XHI * CORES + (halves[done][0]) * XHI * CORES:
            part = pl.ds(halves[done][0], len(halves[done]))
            mail.start(("s1", done), sums.at[1 - core, part], core_got.at[part], cpart)
            done += 1
    assert done == len(halves)
    for n, h in enumerate(halves):
        mail.take(("s1", n), core_got.at[pl.ds(h[0], len(h))], cpart)
    value = (sums[core] + core_got[...]).reshape(depth * XHI * piece, width)
    keep1[...] = value.reshape(keep1.shape)
    peak = jnp.maximum(jnp.max(jnp.abs(value), axis=0, keepdims=True), 1e-30)
    z_scale[...] = peak * (1.0 / TOP)
    z_code[...] = jnp.round(value * (TOP / peak)).astype(jnp.int32).astype(I16).reshape(z_code.shape)
    for c in chips:
        mail.start("s2", z_code.at[(z + c[0]) % depth, xhi ^ c[1]], z_got.at[slot[c]], chip[c])
    for c in chips:
        mail.start("s2s", z_scale, z_sgot.at[slot[c]], chip[c])
    mail.take("s2s", z_sgot, xpart)
    mail.take("s2", z_got, xpart)
    value = keep1[z, xhi]
    for n in range(len(chips)):
        value = value + decode(z_got[n], z_sgot[n])
    last[...] = value
    finished = pltpu.make_async_copy(last, out, load.at[groups + 1])
    finished.start()
    written.wait()
    mail.close(cpart)
    finished.wait()


def call(groups, count, border, inverse, prior, sel, asg, prob):
    size = border.shape[1]
    own, width = prior.shape
    depth = count // (CORES * XHI)
    messages = 59
    n = max(depth - 1, 1)
    others = depth * XHI - 1
    piece = size // count
    high = size // LANES * width
    ny = groups // XLO
    ra, rb = split(own, 0.53)
    dma, vmem = pltpu.SemaphoreType.DMA, pltpu.VMEM
    anyspace = pl.BlockSpec(memory_space=pl.ANY)
    return pl.pallas_call(
        functools.partial(kernel, groups, count),
        out_shape=(jax.ShapeDtypeStruct((own, width), F32), jax.ShapeDtypeStruct((piece, width), F32)),
        in_specs=[anyspace] * 6,
        out_specs=(anyspace, anyspace),
        scratch_shapes=[
            vmem((1, width), jnp.int32),
            pltpu.SMEM((groups,), jnp.int32),
            pltpu.SMEM((groups,), F32),
            vmem((piece, width), F32),
            vmem((groups, own, size), BF16),
            vmem((size, size), BF16),
            vmem((own, width), BF16),
            vmem((high, LANES), BF16),
            vmem((high, LANES), BF16),
            vmem((groups, width, own), BF16),
            vmem((high // CORES, LANES), BF16),
            vmem((others, high // count, LANES), BF16),
            vmem((2 * width, LANES), BF16),
            vmem((2 * width // CORES, LANES), BF16),
            vmem((2 * width // (CORES * XHI), LANES), BF16),
            vmem((n, 2 * width // count, LANES), BF16),
            vmem((2 * width // count, LANES), BF16),
            vmem((groups - 1, 2 * width // count, LANES), BF16),
            vmem((2 * width, LANES), BF16),
            vmem((width, size), BF16),
            vmem((size, width), BF16),
            vmem((width // CORES // min(4, depth), width), F32),
            vmem((groups - 1, width // CORES // min(4, depth), width), F32),
            vmem((width, width), F32),
            vmem((ny, 2, ra, width), I16),
            vmem((ny, 2, 1, width), F32),
            vmem((ny, 2, ra, width), I16),
            vmem((ny, 2, 1, width), F32),
            vmem((ny, rb, width), I16),
            vmem((ny, 1, width), F32),
            vmem((ny, rb, width), I16),
            vmem((ny, 1, width), F32),
            vmem((ra, width), I16),
            vmem((1, width), F32),
            vmem((ra, width), I16),
            vmem((1, width), F32),
            vmem((ny, rb, width), I16),
            vmem((ny, 1, width), F32),
            vmem((ny, rb, width), I16),
            vmem((ny, 1, width), F32),
            vmem((own, width), F32),
            vmem((own, width), F32),
            vmem((ra, width), F32),
            vmem((ny, rb, width), F32),
            vmem((own, width), F32),
            vmem((BASE, 2 * BASE), F32),
            vmem((BASE, BASE), F32),
            vmem((BASE, BASE), F32),
            vmem((BASE, BASE), F32),
            vmem((groups, own, width), BF16),
            vmem((width, size), F32),
            vmem((CORES, depth, XHI, piece, width), F32),
            vmem((depth, XHI, piece, width), F32),
            vmem((depth, XHI, piece, width), F32),
            vmem((depth, XHI, piece, width), I16),
            vmem((1, width), F32),
            vmem((others, piece, width), I16),
            vmem((others, 1, width), F32),
            vmem((3072, LANES), BF16),
            vmem((64, 1, width), F32),
            dma((groups + 5,)),
            dma((12,)),
            dma((messages,)),
        ],
        compiler_params=pltpu.CompilerParams(
            collective_id=0, has_side_effects=True, vmem_limit_bytes=60 << 20
        ),
        name="panel",
    )(border, inverse, prior, sel, asg, prob)


def finish_kernel(panel, residual, panel_out, residual_out, held, kept, came, went):
    rows = panel.shape[0] // 4
    parts = [(panel.at[pl.ds(n * rows, rows)], held.at[n], panel_out.at[pl.ds(n * rows, rows)]) for n in range(4)]
    parts = [(residual, kept, residual_out)] + parts
    ins = [pltpu.make_async_copy(src, mid, came.at[n]) for n, (src, mid, _) in enumerate(parts)]
    outs = [pltpu.make_async_copy(mid, dst, went.at[n]) for n, (_, mid, dst) in enumerate(parts)]
    for go in ins:
        go.start()
    for go, out in zip(ins, outs):
        go.wait()
        out.start()
    for out in outs:
        out.wait()


def finish(panel, residual):
    anyspace = pl.BlockSpec(memory_space=pl.ANY)
    rows, width = panel.shape
    return pl.pallas_call(
        finish_kernel,
        out_shape=(jax.ShapeDtypeStruct(panel.shape, F32), jax.ShapeDtypeStruct(residual.shape, F32)),
        in_specs=[anyspace, anyspace],
        out_specs=(anyspace, anyspace),
        scratch_shapes=[
            pltpu.VMEM((4, rows // 4, width), F32),
            pltpu.VMEM(residual.shape, F32),
            pltpu.SemaphoreType.DMA((5,)),
            pltpu.SemaphoreType.DMA((5,)),
        ],
        name="finish",
    )(panel, residual)


def body(border, inverse_blocks, selected, assignment, probability, prior_panel):
    groups, count = lax.axis_size("grp"), lax.axis_size("dev")
    panel, residual = call(
        groups, count, border[0], inverse_blocks[0], prior_panel, selected[None, :], assignment, probability
    )
    panel, residual = finish(panel, residual)
    return (panel, residual[None])


def solution(mesh):
    return jax.shard_map(
        body,
        mesh=mesh,
        in_specs=(
            P("grp", "dev", None),
            P("grp", None, None),
            P(),
            P(),
            P(),
            P(("dev", "grp"), None),
        ),
        out_specs=(P(("dev", "grp"), None), P("grp", "dev", None)),
        check_vma=False,
    )
```
